32 devices in a mesh: wide: 8 (over z, x), narrow: 4 (over y, core).
Axes of the slice: x: 2, y: 2, z: 4, core: 2. Of those that a mesh axis runs over, the one named last changes fastest.
Arguments:
- table: float32 [256, 256, 64, 128], P(None, 'narrow', 'wide'), may hold values from -200 to 200, as said below
- prior_one: float32 [256, 32], replicated, may hold values from -0.375 to 0.375
- factor_two: float32 [256, 32], replicated, may hold values from -0.375 to 0.375
- factor_three: float32 [64, 32], replicated, may hold values from -0.75 to 0.75
Outputs:
- core: float32 [32, 32, 32, 128], P('narrow', 'wide')
- basis: float32 [256, 32], replicated
The draws below stay inside these ranges and needn't reach their ends.
Inputs may be any that keep to these rules, and one draw needn't show every extreme that they name: Entries of the table lie within the stated bounds.
All inputs are finite; a program needn't handle non-finite values.
Results may differ from the reference program's by a relative error of at most 0.0003.
Values sent between devices are 32-bit elements; how exact they have to be, the bound alone decides.
A program may use at most 256 MiB of HBM per device.

```python
import jax
import jax.numpy as jnp
from jax import lax

I1 = 256
I2 = 256
I3 = 64
M = 128
R = 32
R2 = 32
R3 = 32
SUB = 2


def draw_table(key, part):
    keys = jax.random.split(key, 4)
    rows = jnp.exp(jax.random.uniform(keys[0], (I1, 1, 1, 1), jnp.float32, 0.0, 2.3))
    noise = jax.random.truncated_normal(keys[3], -5.0, 5.0, (I1, I2, I3, M), jnp.float32)
    second = jax.random.uniform(keys[1], (1, I2, 1, 1), jnp.float32, 0.5, 2.0)
    third = jax.random.uniform(keys[2], (1, 1, I3, 1), jnp.float32, 0.5, 2.0)
    return rows * second * third * noise


def bell_draw(own_key, shape, spread, limit, kind=jnp.bfloat16):
    result = spread * jax.random.normal(own_key, shape, jnp.float32)
    return jnp.clip(result, min=-limit, max=limit).astype(kind)


def setup_inputs(seed: int = 0) -> dict:
    streams_of = jax.random.split(jax.random.key(seed), 5)
    table = draw_table(jax.random.fold_in(streams_of[4], 71), 0)
    prior_one = bell_draw(streams_of[1], (I1, R), I1 ** -0.5, 0.375, jnp.float32)
    factor_two = bell_draw(streams_of[2], (I2, R2), I2 ** -0.5, 0.375, jnp.float32)
    factor_three = bell_draw(streams_of[3], (I3, R3), I3 ** -0.5, 0.75, jnp.float32)
    return {"table": table, "prior_one": prior_one, "factor_two": factor_two, "factor_three": factor_three}


HIGH = lax.Precision.HIGHEST

def orthonormal(q):
    s = jnp.dot(q.T.astype(jnp.float32), q.astype(jnp.float32), precision=HIGH, preferred_element_type=jnp.float32)
    lower = jnp.linalg.cholesky(s)
    return lax.linalg.triangular_solve(lower, q, left_side=False, lower=True, transpose_a=True)

def reference(table, prior_one, factor_two, factor_three):
    flat = table.reshape(I1, I2 * I3 * M)
    gram = jnp.dot(flat.astype(jnp.float32), flat.T.astype(jnp.float32), precision=HIGH, preferred_element_type=jnp.float32) / float(I2 * I3 * M)
    basis = prior_one
    for step in range(SUB):
        basis = orthonormal(jnp.dot(gram.astype(jnp.float32), basis.astype(jnp.float32), precision=HIGH, preferred_element_type=jnp.float32))
    cut_off = jnp.dot(basis.T.astype(jnp.float32), flat.astype(jnp.float32), precision=HIGH, preferred_element_type=jnp.float32).reshape(R, I2, I3, M)
    second = jnp.einsum('aijm,ib->abjm', cut_off, factor_two, precision=HIGH)
    core = jnp.einsum('abjm,jc->abcm', second, factor_three, precision=HIGH)
    return (core, basis)
```

```python
import functools

import jax
import jax.numpy as jnp
from jax import lax
from jax.experimental import pallas as pl
from jax.experimental.pallas import tpu as pltpu
from jax.sharding import PartitionSpec as P

I2 = 256
I3 = 64
M = 128
SUB = 2

F32 = jnp.float32
BF16 = jnp.bfloat16
HIGH = lax.Precision.HIGHEST
NT = (((1,), (1,)), ((), ()))
TN = (((0,), (0,)), ((), ()))
MESH = pl.DeviceIdType.MESH


def split(x):
    hi = x.astype(BF16)
    return hi, (x - hi.astype(F32)).astype(BF16)


def gather_rows(ref, first, group):
    block = jnp.swapaxes(ref[:, pl.ds(pl.multiple_of(first, group), group), :], 0, 1)
    return jnp.concatenate([block[t] for t in range(group)], axis=1)


SUBLANES = 8
DEPTH = 3


def gram_kernel(block, group, table_ref, gram_ref, buf, acc, cross, sems):
    tall, lines, rows, cells = table_ref.shape
    padded = buf.shape[3]
    steps = rows // block
    acc[...] = jnp.zeros_like(acc)
    cross[...] = jnp.zeros_like(cross)

    def fetch(i, slot):
        first = pl.multiple_of(i * block, block)
        return [
            pltpu.make_async_copy(
                table_ref.at[:, s, pl.ds(first, block), :],
                buf.at[slot, s, :, pl.ds(s, block), :],
                sems.at[slot, s],
            )
            for s in range(lines)
        ]

    for i in range(min(DEPTH - 1, steps)):
        for copy in fetch(i, i):
            copy.start()
    flat = buf.reshape(DEPTH * lines * tall * padded, cells)
    stride = tall * padded + 1

    def body(i, carry):
        slot = lax.rem(i, DEPTH)
        ahead = i + DEPTH - 1

        @pl.when(ahead < steps)
        def _():
            for copy in fetch(ahead, lax.rem(ahead, DEPTH)):
                copy.start()

        for copy in fetch(i, slot):
            copy.wait()
        base = slot * (lines * tall * padded)

        def part(g, carry):
            columns = []
            for t in range(group):
                at = base + g * group + t
                columns.append(
                    jnp.concatenate(
                        [flat[pl.ds(at + q * padded, lines, stride=stride), :] for q in range(tall)],
                        axis=0,
                    )
                )
            hi, lo = split(jnp.concatenate(columns, axis=1))
            acc[...] += lax.dot_general(hi, hi, NT, preferred_element_type=F32)
            cross[...] += lax.dot_general(hi, lo, NT, preferred_element_type=F32)
            return carry

        return lax.fori_loop(0, block // group, part, carry)

    lax.fori_loop(0, steps, body, 0)
    gram_ref[...] = acc[...] + (cross[...] + cross[...].T)


def gram_of(flat):
    order, rows, cells = flat.shape
    block = min(32, rows)
    tall = order // SUBLANES
    return pl.pallas_call(
        functools.partial(gram_kernel, block, min(16, block)),
        in_specs=[pl.BlockSpec(memory_space=pl.ANY)],
        out_specs=pl.BlockSpec(memory_space=pltpu.VMEM),
        out_shape=jax.ShapeDtypeStruct((order, order), F32),
        scratch_shapes=[
            pltpu.VMEM((DEPTH, SUBLANES, tall, block + SUBLANES, cells), F32),
            pltpu.VMEM((order, order), F32),
            pltpu.VMEM((order, order), F32),
            pltpu.SemaphoreType.DMA((DEPTH, SUBLANES)),
        ],
        compiler_params=pltpu.CompilerParams(vmem_limit_bytes=48 << 20),
    )(flat.reshape(tall, SUBLANES, rows, cells))


def greet(narrow, wide, at, place):
    barrier = pltpu.get_barrier_semaphore()
    for d in range(1, narrow):
        pl.semaphore_signal(
            barrier, inc=1, device_id={"narrow": lax.rem(at + d, narrow)}, device_id_type=MESH
        )
    for d in range(1, wide):
        pl.semaphore_signal(
            barrier, inc=1, device_id={"wide": lax.rem(place + d, wide)}, device_id_type=MESH
        )


def send(src, dst, send_sem, recv_sem, axis, to):
    copy = pltpu.make_async_remote_copy(
        src_ref=src,
        dst_ref=dst,
        send_sem=send_sem,
        recv_sem=recv_sem,
        device_id={axis: to},
        device_id_type=MESH,
    )
    copy.start()
    return copy


def finish(copies):
    for copy in copies:
        copy.wait()


def basis_kernel(
    narrow, wide, scale, part_ref, prior_ref, turned_ref,
    box_n, mine, box_w, full, square, sn, rn, sw, rw, tw, vw, tn, vn,
):
    at, place = lax.axis_index("narrow"), lax.axis_index("wide")
    greet(narrow, wide, at, place)
    pl.semaphore_wait(pltpu.get_barrier_semaphore(), narrow + wide - 2)
    copies = []
    for d in range(1, narrow):
        to = lax.rem(at + d, narrow)
        copies.append(send(part_ref.at[to], box_n.at[d], sn.at[d], rn.at[d], "narrow", to))
    finish(copies)
    value = part_ref[at]
    for d in range(1, narrow):
        value = value + box_n[d]
    mine[...] = value
    copies = []
    for d in range(1, wide):
        to = lax.rem(place + d, wide)
        copies.append(send(mine.at[to], box_w.at[d], sw.at[d], rw.at[d], "wide", to))
    finish(copies)
    value = mine[place]
    for d in range(1, wide):
        value = value + box_w[d]
    full[at, place] = value * scale
    copies = []
    for d in range(1, wide):
        to = lax.rem(place + d, wide)
        own = full.at[at, place]
        copies.append(send(own, own, tw.at[d], vw.at[d], "wide", to))
    finish(copies)
    copies = []
    for d in range(1, narrow):
        to = lax.rem(at + d, narrow)
        own = full.at[at]
        copies.append(send(own, own, tn.at[d], vn.at[d], "narrow", to))
    finish(copies)
    small = full.shape[2]
    for i in range(narrow * wide):
        square[i * small : (i + 1) * small, :] = full[i // wide, i % wide]
    gram = square[...]
    basis = prior_ref[...].T
    rank = basis.shape[1]
    row = lax.broadcasted_iota(jnp.int32, (rank, 1), 0)
    lane = lax.broadcasted_iota(jnp.int32, (rank, rank), 1)
    unit = jnp.where(lane == lax.broadcasted_iota(jnp.int32, (rank, rank), 0), 1.0, 0.0)
    for _ in range(SUB):
        q = jnp.dot(gram, basis, precision=HIGH, preferred_element_type=F32)
        s = lax.dot_general(q, q, TN, precision=HIGH, preferred_element_type=F32)
        pair = jnp.concatenate([s, unit], axis=1)
        root = jnp.ones((rank, 1), F32)
        for k in range(rank):
            line = pair[k : k + 1, :]
            pivot = line[:, k : k + 1]
            root = jnp.where(row == k, pivot, root)
            factor = jnp.where(row > k, pair[:, k : k + 1], 0.0)
            pair = pair - factor * (line / pivot)
        inverse = pair[:, rank:] * lax.rsqrt(root)
        basis = lax.dot_general(q, inverse, NT, precision=HIGH, preferred_element_type=F32)
    turned_ref[...] = basis.T


def basis_of(narrow, wide, gram, prior):
    scale = 1.0 / float(I2 * I3 * M)
    order, rank = prior.shape
    small = order // (narrow * wide)
    dma = pltpu.SemaphoreType.DMA
    return pl.pallas_call(
        functools.partial(basis_kernel, narrow, wide, scale),
        in_specs=[pl.BlockSpec(memory_space=pltpu.VMEM)] * 2,
        out_specs=pl.BlockSpec(memory_space=pltpu.VMEM),
        out_shape=jax.ShapeDtypeStruct((rank, order), F32),
        scratch_shapes=[
            pltpu.VMEM((narrow, wide, small, order), F32),
            pltpu.VMEM((wide, small, order), F32),
            pltpu.VMEM((wide, small, order), F32),
            pltpu.VMEM((narrow, wide, small, order), F32),
            pltpu.VMEM((order, order), F32),
            dma((narrow,)), dma((narrow,)),
            dma((wide,)), dma((wide,)),
            dma((wide,)), dma((wide,)),
            dma((narrow,)), dma((narrow,)),
        ],
        compiler_params=pltpu.CompilerParams(collective_id=1, has_side_effects=True),
    )(gram.reshape(narrow, wide, small, order), prior.T)


def project_kernel(
    group, depth, narrow, wide, spread, turned_ref, two_ref, table_ref, out_ref,
    trunc, second, core_box, chip_box, wide_box, sc, rc, sy, ry, sw, rw,
):
    _, rows, cells = table_ref.shape
    rank = turned_ref.shape[0]
    total = trunc.shape[0] // rank
    tall = total // depth
    step = pl.program_id(0)
    at, place = lax.axis_index("narrow"), lax.axis_index("wide")

    @pl.when(step == 0)
    def _():
        greet(narrow, wide, at, place)

    left_hi, left_lo = split(turned_ref[...])
    left = jnp.concatenate([left_hi, left_lo], axis=0)

    def body(g, carry):
        hi, lo = split(gather_rows(table_ref, g * group, group))
        both = jnp.dot(left, hi, preferred_element_type=F32)
        value = both[:rank] + (both[rank:] + jnp.dot(left_hi, lo, preferred_element_type=F32))
        for t in range(group):
            spot = step * rows + g * group + t
            spot = lax.rem(spot, depth) * tall + spot // depth
            trunc[pl.ds(spot, rank, stride=total), :] = value[:, t * cells : (t + 1) * cells]
        return carry

    lax.fori_loop(0, rows // group, body, 0)

    @pl.when(step == pl.num_programs(0) - 1)
    def _():
        pl.semaphore_wait(pltpu.get_barrier_semaphore(), narrow + wide - 2)
        two_hi, two_lo = split(two_ref[...])
        two = jnp.concatenate([two_hi, two_lo], axis=0)
        width = two_ref.shape[0]
        per = rank // narrow
        slab = width * depth
        chips = narrow // 2
        chip, core = at // 2, lax.rem(at, 2)
        chunk, chunks = 1, per
        flat = second.reshape(rank * slab, cells)

        def compute(block, q):
            def one(k, carry):
                r = block * per + q * chunk + k
                parts = [
                    trunc[pl.ds(pl.multiple_of(r * total + j * tall, tall), tall), :]
                    for j in range(depth)
                ]
                hi, lo = split(jnp.concatenate(parts, axis=1))
                both = jnp.dot(two, hi, preferred_element_type=F32)
                value = both[:width] + (
                    both[width:] + jnp.dot(two_hi, lo, preferred_element_type=F32)
                )
                for j in range(depth):
                    flat[pl.ds(r * slab + j, width, stride=depth), :] = value[
                        :, j * cells : (j + 1) * cells
                    ]
                return carry

            lax.fori_loop(0, chunk, one, 0)

        def part(q):
            return pl.ds(q * chunk, chunk)

        def target(h):
            return lax.rem(chip + h, chips)

        to_core, to_chip, to_wide = {}, {}, []

        def start(h, q):
            other = target(h) * 2 + (1 - core)
            compute(other, q)
            to_core[h, q] = send(
                second.at[other, part(q)], core_box.at[h, part(q)],
                sc.at[h, q], rc.at[h, q], "narrow", chip * 2 + (1 - core),
            )
            compute(target(h) * 2 + core, q)

        def merge(h, q):
            to_core[h, q].wait_recv()
            block = target(h) * 2 + core
            second[block, part(q)] = second[block, part(q)] + core_box[h, part(q)]
            if h:
                to_chip[h, q] = send(
                    second.at[block, part(q)], chip_box.at[h - 1, part(q)],
                    sy.at[h, q], ry.at[h, q], "narrow", block,
                )

        pairs = [(h, q) for h in [*range(1, chips), 0] for q in range(chunks)]
        for i, pair in enumerate(pairs):
            start(*pair)
            if i:
                merge(*pairs[i - 1])
        merge(*pairs[-1])
        for q in range(chunks):
            value = second[at, part(q)]
            for h in range(1, chips):
                to_chip[h, q].wait_recv()
                value = value + chip_box[h - 1, part(q)]
            if not spread:
                out_ref[0, part(q)] = value
                continue
            second[at, part(q)] = value
            band = slab // wide
            for d in range(1, wide):
                to = lax.rem(place + d, wide)
                rows_to = pl.ds(pl.multiple_of(to * band, band), band)
                to_wide.append(
                    send(
                        second.at[at, part(q), rows_to], wide_box.at[place, part(q)],
                        sw.at[d, q], rw.at[d, q], "wide", to,
                    )
                )
            own = pl.ds(pl.multiple_of(place * band, band), band)
            out_ref[place, part(q)] = second[at, part(q), own]
        for copy in [*to_core.values(), *to_chip.values()]:
            copy.wait_send()
        finish(to_wide)
        if spread:
            for d in range(1, wide):
                source = lax.rem(place + d, wide)
                out_ref[source] = wide_box[source]


def project(narrow, wide, turned, two, flat, depth):
    order, rows, cells = flat.shape
    rank, width = turned.shape[0], two.shape[0]
    block = min(32, rows)
    per, slab, chips = rank // narrow, width * depth, narrow // 2
    spread = (slab // wide) % 8 == 0
    shape = (wide, per, slab // wide, cells) if spread else (1, per, slab, cells)
    chunks = per
    dma = pltpu.SemaphoreType.DMA
    out = pl.pallas_call(
        functools.partial(
            project_kernel, min(16, block), depth, narrow, wide, spread
        ),
        grid=(rows // block,),
        in_specs=[
            pl.BlockSpec(turned.shape, lambda i: (0, 0)),
            pl.BlockSpec(two.shape, lambda i: (0, 0)),
            pl.BlockSpec((order, block, cells), lambda i: (0, i, 0)),
        ],
        out_specs=pl.BlockSpec(shape, lambda i: (0, 0, 0, 0)),
        out_shape=jax.ShapeDtypeStruct(shape, F32),
        scratch_shapes=[
            pltpu.VMEM((rank * rows, cells), F32),
            pltpu.VMEM((narrow, per, slab, cells), F32),
            pltpu.VMEM((chips, per, slab, cells), F32),
            pltpu.VMEM((max(chips - 1, 1), per, slab, cells), F32),
            pltpu.VMEM(shape, F32),
            dma((chips, chunks)), dma((chips, chunks)),
            dma((chips, chunks)), dma((chips, chunks)),
            dma((wide, chunks)), dma((wide, chunks)),
        ],
        compiler_params=pltpu.CompilerParams(
            vmem_limit_bytes=56 << 20, collective_id=2, has_side_effects=True
        ),
    )(turned, two, flat)
    if not spread:
        out = out.reshape(per, wide, slab // wide, cells)
        out = lax.all_to_all(out, "wide", split_axis=1, concat_axis=1, tiled=True)
        out = out.transpose(1, 0, 2, 3)
    return out.reshape(wide, per, width // wide, depth, cells)


def per_device(narrow, wide, table, prior_one, factor_two, factor_three):
    order, rows_two, rows_three, cells = table.shape
    flat = table.reshape(order, rows_two * rows_three, cells)
    turned = basis_of(narrow, wide, gram_of(flat), prior_one)
    at = lax.axis_index("narrow")
    two = lax.dynamic_slice_in_dim(factor_two, at * rows_two, rows_two, 0).T
    spread = project(narrow, wide, turned, two, flat, rows_three)
    three = factor_three.reshape(wide, rows_three, factor_three.shape[1])
    core_out = jnp.einsum("wrbjm,wjc->rbcm", spread, three, precision=HIGH)
    return core_out, turned.T


def solution(mesh):
    return jax.shard_map(
        functools.partial(per_device, mesh.shape["narrow"], mesh.shape["wide"]),
        mesh=mesh,
        in_specs=(P(None, "narrow", "wide", None), P(), P(), P()),
        out_specs=(P("narrow", "wide", None, None), P()),
        check_vma=False,
    )
```

```python
import functools

import jax
import jax.numpy as jnp
from jax import lax
from jax.experimental import pallas as pl
from jax.experimental.pallas import tpu as pltpu
from jax.sharding import PartitionSpec as P

I2 = 256
I3 = 64
M = 128
SUB = 2

F32 = jnp.float32
BF16 = jnp.bfloat16
HIGH = lax.Precision.HIGHEST
NT = (((1,), (1,)), ((), ()))
TN = (((0,), (0,)), ((), ()))
MESH = pl.DeviceIdType.MESH


def split(x):
    hi = x.astype(BF16)
    return hi, (x - hi.astype(F32)).astype(BF16)


def gather_rows(ref, first, group):
    block = jnp.swapaxes(ref[:, pl.ds(pl.multiple_of(first, group), group), :], 0, 1)
    return jnp.concatenate([block[t] for t in range(group)], axis=1)


SUBLANES = 8
DEPTH = 3


def gram_kernel(block, group, table_ref, gram_ref, buf, acc, cross, sems):
    tall, lines, rows, cells = table_ref.shape
    padded = buf.shape[3]
    steps = rows // block
    acc[...] = jnp.zeros_like(acc)
    cross[...] = jnp.zeros_like(cross)

    def fetch(i, slot):
        first = pl.multiple_of(i * block, block)
        return [
            pltpu.make_async_copy(
                table_ref.at[:, s, pl.ds(first, block), :],
                buf.at[slot, s, :, pl.ds(s, block), :],
                sems.at[slot, s],
            )
            for s in range(lines)
        ]

    for i in range(min(DEPTH - 1, steps)):
        for copy in fetch(i, i):
            copy.start()
    flat = buf.reshape(DEPTH * lines * tall * padded, cells)
    stride = tall * padded + 1

    def body(i, carry):
        slot = lax.rem(i, DEPTH)
        ahead = i + DEPTH - 1

        @pl.when(ahead < steps)
        def _():
            for copy in fetch(ahead, lax.rem(ahead, DEPTH)):
                copy.start()

        for copy in fetch(i, slot):
            copy.wait()
        base = slot * (lines * tall * padded)

        def part(g, carry):
            columns = []
            for t in range(group):
                at = base + g * group + t
                columns.append(
                    jnp.concatenate(
                        [flat[pl.ds(at + q * padded, lines, stride=stride), :] for q in range(tall)],
                        axis=0,
                    )
                )
            hi, lo = split(jnp.concatenate(columns, axis=1))
            acc[...] += lax.dot_general(hi, hi, NT, preferred_element_type=F32)
            cross[...] += lax.dot_general(hi, lo, NT, preferred_element_type=F32)
            return carry

        return lax.fori_loop(0, block // group, part, carry)

    lax.fori_loop(0, steps, body, 0)
    gram_ref[...] = acc[...] + (cross[...] + cross[...].T)


def gram_of(flat):
    order, rows, cells = flat.shape
    block = min(32, rows)
    tall = order // SUBLANES
    return pl.pallas_call(
        functools.partial(gram_kernel, block, min(16, block)),
        in_specs=[pl.BlockSpec(memory_space=pl.ANY)],
        out_specs=pl.BlockSpec(memory_space=pltpu.VMEM),
        out_shape=jax.ShapeDtypeStruct((order, order), F32),
        scratch_shapes=[
            pltpu.VMEM((DEPTH, SUBLANES, tall, block + SUBLANES, cells), F32),
            pltpu.VMEM((order, order), F32),
            pltpu.VMEM((order, order), F32),
            pltpu.SemaphoreType.DMA((DEPTH, SUBLANES)),
        ],
        compiler_params=pltpu.CompilerParams(vmem_limit_bytes=48 << 20),
    )(flat.reshape(tall, SUBLANES, rows, cells))


def greet(narrow, wide, at, place):
    barrier = pltpu.get_barrier_semaphore()
    for d in range(1, narrow):
        pl.semaphore_signal(
            barrier, inc=1, device_id={"narrow": lax.rem(at + d, narrow)}, device_id_type=MESH
        )
    for d in range(1, wide):
        pl.semaphore_signal(
            barrier, inc=1, device_id={"wide": lax.rem(place + d, wide)}, device_id_type=MESH
        )


def send(src, dst, send_sem, recv_sem, axis, to):
    copy = pltpu.make_async_remote_copy(
        src_ref=src,
        dst_ref=dst,
        send_sem=send_sem,
        recv_sem=recv_sem,
        device_id={axis: to},
        device_id_type=MESH,
    )
    copy.start()
    return copy


def finish(copies):
    for copy in copies:
        copy.wait()


def basis_from(gram, prior):
    basis = prior.T
    rank = basis.shape[1]
    row = lax.broadcasted_iota(jnp.int32, (rank, 1), 0)
    lane = lax.broadcasted_iota(jnp.int32, (rank, rank), 1)
    unit = jnp.where(lane == lax.broadcasted_iota(jnp.int32, (rank, rank), 0), 1.0, 0.0)
    for _ in range(SUB):
        q = jnp.dot(gram, basis, precision=HIGH, preferred_element_type=F32)
        s = lax.dot_general(q, q, TN, precision=HIGH, preferred_element_type=F32)
        pair = jnp.concatenate([s, unit], axis=1)
        root = jnp.ones((rank, 1), F32)
        for k in range(rank):
            line = pair[k : k + 1, :]
            pivot = line[:, k : k + 1]
            root = jnp.where(row == k, pivot, root)
            factor = jnp.where(row > k, pair[:, k : k + 1], 0.0)
            pair = pair - factor * (line / pivot)
        inverse = pair[:, rank:] * lax.rsqrt(root)
        basis = lax.dot_general(q, inverse, NT, precision=HIGH, preferred_element_type=F32)
    return basis.T


def basis_kernel(
    narrow, wide, scale, part_ref, prior_ref, turned_ref,
    box_n, mine, box_w, full, square, sn, rn, sw, rw, tw, vw, tn, vn,
):
    at, place = lax.axis_index("narrow"), lax.axis_index("wide")
    greet(narrow, wide, at, place)
    pl.semaphore_wait(pltpu.get_barrier_semaphore(), narrow + wide - 2)
    copies = []
    for d in range(1, narrow):
        to = lax.rem(at + d, narrow)
        copies.append(send(part_ref.at[to], box_n.at[d], sn.at[d], rn.at[d], "narrow", to))
    finish(copies)
    value = part_ref[at]
    for d in range(1, narrow):
        value = value + box_n[d]
    mine[...] = value
    copies = []
    for d in range(1, wide):
        to = lax.rem(place + d, wide)
        copies.append(send(mine.at[to], box_w.at[d], sw.at[d], rw.at[d], "wide", to))
    finish(copies)
    value = mine[place]
    for d in range(1, wide):
        value = value + box_w[d]
    full[at, place] = value * scale
    copies = []
    for d in range(1, wide):
        to = lax.rem(place + d, wide)
        own = full.at[at, place]
        copies.append(send(own, own, tw.at[d], vw.at[d], "wide", to))
    finish(copies)
    copies = []
    for d in range(1, narrow):
        to = lax.rem(at + d, narrow)
        own = full.at[at]
        copies.append(send(own, own, tn.at[d], vn.at[d], "narrow", to))
    finish(copies)
    small = full.shape[2]
    for i in range(narrow * wide):
        square[i * small : (i + 1) * small, :] = full[i // wide, i % wide]
    gram = square[...]
    turned_ref[...] = basis_from(gram, prior_ref[...])


def basis_of(narrow, wide, gram, prior):
    scale = 1.0 / float(I2 * I3 * M)
    order, rank = prior.shape
    small = order // (narrow * wide)
    dma = pltpu.SemaphoreType.DMA
    return pl.pallas_call(
        functools.partial(basis_kernel, narrow, wide, scale),
        in_specs=[pl.BlockSpec(memory_space=pltpu.VMEM)] * 2,
        out_specs=pl.BlockSpec(memory_space=pltpu.VMEM),
        out_shape=jax.ShapeDtypeStruct((rank, order), F32),
        scratch_shapes=[
            pltpu.VMEM((narrow, wide, small, order), F32),
            pltpu.VMEM((wide, small, order), F32),
            pltpu.VMEM((wide, small, order), F32),
            pltpu.VMEM((narrow, wide, small, order), F32),
            pltpu.VMEM((order, order), F32),
            dma((narrow,)), dma((narrow,)),
            dma((wide,)), dma((wide,)),
            dma((wide,)), dma((wide,)),
            dma((narrow,)), dma((narrow,)),
        ],
        compiler_params=pltpu.CompilerParams(collective_id=1, has_side_effects=True),
    )(gram.reshape(narrow, wide, small, order), prior.T)


def project_kernel(
    group, depth, narrow, wide, spread, turned_ref, two_ref, table_ref, out_ref,
    trunc, second, core_box, chip_box, wide_box, sc, rc, sy, ry, sw, rw,
):
    _, rows, cells = table_ref.shape
    rank = turned_ref.shape[0]
    total = trunc.shape[0] // rank
    tall = total // depth
    step = pl.program_id(0)
    at, place = lax.axis_index("narrow"), lax.axis_index("wide")

    @pl.when(step == 0)
    def _():
        greet(narrow, wide, at, place)

    left_hi, left_lo = split(turned_ref[...])
    left = jnp.concatenate([left_hi, left_lo], axis=0)

    def body(g, carry):
        hi, lo = split(gather_rows(table_ref, g * group, group))
        both = jnp.dot(left, hi, preferred_element_type=F32)
        value = both[:rank] + (both[rank:] + jnp.dot(left_hi, lo, preferred_element_type=F32))
        for t in range(group):
            spot = step * rows + g * group + t
            spot = lax.rem(spot, depth) * tall + spot // depth
            trunc[pl.ds(spot, rank, stride=total), :] = value[:, t * cells : (t + 1) * cells]
        return carry

    lax.fori_loop(0, rows // group, body, 0)

    @pl.when(step == pl.num_programs(0) - 1)
    def _():
        pl.semaphore_wait(pltpu.get_barrier_semaphore(), narrow + wide - 2)
        two_hi, two_lo = split(two_ref[...])
        two = jnp.concatenate([two_hi, two_lo], axis=0)
        width = two_ref.shape[0]
        per = rank // narrow
        slab = width * depth
        chips = narrow // 2
        chip, core = at // 2, lax.rem(at, 2)
        chunk, chunks = 1, per
        flat = second.reshape(rank * slab, cells)

        def compute(block, q):
            def one(k, carry):
                r = block * per + q * chunk + k
                parts = [
                    trunc[pl.ds(pl.multiple_of(r * total + j * tall, tall), tall), :]
                    for j in range(depth)
                ]
                hi, lo = split(jnp.concatenate(parts, axis=1))
                both = jnp.dot(two, hi, preferred_element_type=F32)
                value = both[:width] + (
                    both[width:] + jnp.dot(two_hi, lo, preferred_element_type=F32)
                )
                for j in range(depth):
                    flat[pl.ds(r * slab + j, width, stride=depth), :] = value[
                        :, j * cells : (j + 1) * cells
                    ]
                return carry

            lax.fori_loop(0, chunk, one, 0)

        def part(q):
            return pl.ds(q * chunk, chunk)

        def target(h):
            return lax.rem(chip + h, chips)

        to_core, to_chip, to_wide = {}, {}, []

        def start(h, q):
            other = target(h) * 2 + (1 - core)
            compute(other, q)
            to_core[h, q] = send(
                second.at[other, part(q)], core_box.at[h, part(q)],
                sc.at[h, q], rc.at[h, q], "narrow", chip * 2 + (1 - core),
            )
            compute(target(h) * 2 + core, q)

        def merge(h, q):
            to_core[h, q].wait_recv()
            block = target(h) * 2 + core
            second[block, part(q)] = second[block, part(q)] + core_box[h, part(q)]
            if h:
                to_chip[h, q] = send(
                    second.at[block, part(q)], chip_box.at[h - 1, part(q)],
                    sy.at[h, q], ry.at[h, q], "narrow", block,
                )

        pairs = [(h, q) for h in [*range(1, chips), 0] for q in range(chunks)]
        for i, pair in enumerate(pairs):
            start(*pair)
            if i:
                merge(*pairs[i - 1])
        merge(*pairs[-1])
        for q in range(chunks):
            value = second[at, part(q)]
            for h in range(1, chips):
                to_chip[h, q].wait_recv()
                value = value + chip_box[h - 1, part(q)]
            if not spread:
                out_ref[0, part(q)] = value
                continue
            second[at, part(q)] = value
            band = slab // wide
            for d in range(1, wide):
                to = lax.rem(place + d, wide)
                rows_to = pl.ds(pl.multiple_of(to * band, band), band)
                to_wide.append(
                    send(
                        second.at[at, part(q), rows_to], wide_box.at[place, part(q)],
                        sw.at[d, q], rw.at[d, q], "wide", to,
                    )
                )
            own = pl.ds(pl.multiple_of(place * band, band), band)
            out_ref[place, part(q)] = second[at, part(q), own]
        for copy in [*to_core.values(), *to_chip.values()]:
            copy.wait_send()
        finish(to_wide)
        if spread:
            for d in range(1, wide):
                source = lax.rem(place + d, wide)
                out_ref[source] = wide_box[source]


def project(narrow, wide, turned, two, flat, depth):
    order, rows, cells = flat.shape
    rank, width = turned.shape[0], two.shape[0]
    block = min(32, rows)
    per, slab, chips = rank // narrow, width * depth, narrow // 2
    spread = (slab // wide) % 8 == 0
    shape = (wide, per, slab // wide, cells) if spread else (1, per, slab, cells)
    chunks = per
    dma = pltpu.SemaphoreType.DMA
    out = pl.pallas_call(
        functools.partial(
            project_kernel, min(16, block), depth, narrow, wide, spread
        ),
        grid=(rows // block,),
        in_specs=[
            pl.BlockSpec(turned.shape, lambda i: (0, 0)),
            pl.BlockSpec(two.shape, lambda i: (0, 0)),
            pl.BlockSpec((order, block, cells), lambda i: (0, i, 0)),
        ],
        out_specs=pl.BlockSpec(shape, lambda i: (0, 0, 0, 0)),
        out_shape=jax.ShapeDtypeStruct(shape, F32),
        scratch_shapes=[
            pltpu.VMEM((rank * rows, cells), F32),
            pltpu.VMEM((narrow, per, slab, cells), F32),
            pltpu.VMEM((chips, per, slab, cells), F32),
            pltpu.VMEM((max(chips - 1, 1), per, slab, cells), F32),
            pltpu.VMEM(shape, F32),
            dma((chips, chunks)), dma((chips, chunks)),
            dma((chips, chunks)), dma((chips, chunks)),
            dma((wide, chunks)), dma((wide, chunks)),
        ],
        compiler_params=pltpu.CompilerParams(
            vmem_limit_bytes=56 << 20, collective_id=2, has_side_effects=True
        ),
    )(turned, two, flat)
    if not spread:
        out = out.reshape(per, wide, slab // wide, cells)
        out = lax.all_to_all(out, "wide", split_axis=1, concat_axis=1, tiled=True)
        out = out.transpose(1, 0, 2, 3)
    return out.reshape(wide, per, width // wide, depth, cells)


RING = 6
PARTS = 4
WINDOW = (1, 5, 5, 1)
AHEAD = (13, 14, 17, 20, 24, 28, 32, 32)


def fused_kernel(
    narrow, wide, scale,
    table_ref, view_ref, prior_hbm, two_hbm, three_hbm, turned_ref, out_ref,
    prior, wholetwo, three, main, ring, acc, cross, mine, half_box, full, second,
    core_box, chip_box, wide_box, total,
    small_sem, gram_sem, ring_sem, s1, v1, s2, v2, s3, v3, s4, v4, sc, rc, sy, ry, sw, rw,
):
    tall, lines, rows, cells = table_ref.shape
    order, rows_two, depth, _ = view_ref.shape
    rank, width = prior_hbm.shape[0], two_hbm.shape[0]
    slots, _, padded, _ = main.shape
    block = padded - lines
    steps = rows // block
    at, place = lax.axis_index("narrow"), lax.axis_index("wide")
    chips = narrow // 2
    chip, core = at // 2, lax.rem(at, 2)
    groups = chips * wide
    group = chip * wide + place
    twin = {"narrow": chip * 2 + (1 - core)}

    def peer(d):
        to = lax.rem(group + d, groups)
        return to, {"narrow": (to // wide) * 2 + core, "wide": lax.rem(to, wide)}

    barrier = pltpu.get_barrier_semaphore()
    pl.semaphore_signal(barrier, inc=1, device_id=twin, device_id_type=MESH)
    for d in range(1, groups):
        pl.semaphore_signal(barrier, inc=1, device_id=peer(d)[1], device_id_type=MESH)

    small = [
        pltpu.make_async_copy(prior_hbm, prior, small_sem.at[0]),
        pltpu.make_async_copy(two_hbm, wholetwo, small_sem.at[1]),
        pltpu.make_async_copy(three_hbm, three, small_sem.at[2]),
    ]

    first_slot = slots - DEPTH * lines

    def fetch(i, slot):
        first = pl.multiple_of(i * block, block)
        return [
            pltpu.make_async_copy(
                table_ref.at[:, s, pl.ds(first, block), :],
                main.at[first_slot + slot * lines + s, :, pl.ds(s, block), :],
                gram_sem.at[slot, s],
            )
            for s in range(lines)
        ]

    share = order // PARTS
    pieces = depth * PARTS

    def piece(i, slot):
        first = pl.multiple_of(lax.rem(i, PARTS) * share, share)
        return pltpu.make_async_copy(
            view_ref.at[pl.ds(first, share), :, i // PARTS, :], ring.at[slot], ring_sem.at[slot]
        )

    for i in range(DEPTH - 1):
        for copy in fetch(i, i):
            copy.start()
    for copy in small:
        copy.start()
    acc[...] = jnp.zeros_like(acc)
    cross[...] = jnp.zeros_like(cross)
    flat = main.reshape(slots * tall * padded, cells)
    gather = tall * padded + 1
    lane_group = 16

    def gram_step(i, carry):
        slot = lax.rem(i, DEPTH)
        ahead = i + DEPTH - 1

        @pl.when(ahead < steps)
        def _():
            for copy in fetch(ahead, lax.rem(ahead, DEPTH)):
                copy.start()

        @pl.when(i == steps - 2)
        def _():
            for k in range(RING):
                piece(k, k).start()

        for copy in fetch(i, slot):
            copy.wait()
        base = (first_slot + slot * lines) * (tall * padded)

        def part(g, carry):
            columns = []
            for t in range(lane_group):
                spot = base + g * lane_group + t
                columns.append(
                    jnp.concatenate(
                        [flat[pl.ds(spot + q * padded, lines, stride=gather), :] for q in range(tall)],
                        axis=0,
                    )
                )
            hi, lo = split(jnp.concatenate(columns, axis=1))
            acc[...] += lax.dot_general(hi, hi, NT, preferred_element_type=F32)
            cross[...] += lax.dot_general(hi, lo, NT, preferred_element_type=F32)
            return carry

        return lax.fori_loop(0, block // lane_group, part, carry)

    lax.fori_loop(0, steps, gram_step, 0)
    for copy in small:
        copy.wait()

    narrowed = jnp.zeros((width, rows_two), F32)
    for d in range(narrow):
        narrowed = jnp.where(at == d, wholetwo[:, d * rows_two : (d + 1) * rows_two], narrowed)
    two_hi, two_lo = split(narrowed)
    two = jnp.concatenate([two_hi, two_lo], axis=0)
    skew = order + 1
    z_group = 64

    def reduce_piece(i, carry):
        slot = lax.rem(i, RING)
        piece(i, slot).wait()
        base = (i // PARTS) * (width * skew) + lax.rem(i, PARTS) * share

        def one(k, carry):
            hi, lo = split(
                jnp.concatenate([ring[slot, k * z_group + t] for t in range(z_group)], axis=1)
            )
            both = jnp.dot(two, hi, preferred_element_type=F32)
            value = both[:width] + (both[width:] + jnp.dot(two_hi, lo, preferred_element_type=F32))
            for t in range(z_group):
                flat[pl.ds(base + k * z_group + t, width, stride=skew), :] = value[
                    :, t * cells : (t + 1) * cells
                ]
            return carry

        lax.fori_loop(0, share // z_group, one, 0)

        @pl.when(i + RING < pieces)
        def _():
            piece(i + RING, slot).start()

        return carry

    state = [0]

    def advance(to):
        to = min(to, pieces)
        if to > state[0]:
            lax.fori_loop(state[0], to, reduce_piece, 0)
            state[0] = to

    def remote(src, dst, send_sem, recv_sem, to):
        copy = pltpu.make_async_remote_copy(
            src_ref=src, dst_ref=dst, send_sem=send_sem, recv_sem=recv_sem,
            device_id=to, device_id_type=MESH,
        )
        copy.start()
        return copy

    part = acc[...] + (cross[...] + cross[...].T)
    eight = order // (2 * groups)
    for c in range(2):
        for g in range(groups):
            first = (c * groups + g) * eight
            mine[c, g] = part[first : first + eight]
    pl.semaphore_wait(barrier, groups)
    exchange = remote(mine.at[1 - core], full.at[1 - core], s1.at[0], v1.at[0], twin)
    advance(WINDOW[0])
    exchange.wait()
    mine[core] = mine[core] + full[core]
    for d in range(1, groups):
        to, where = peer(d)
        remote(mine.at[core, to], half_box.at[d], s2.at[0], v2.at[0], where)
    advance(sum(WINDOW[:2]))
    others = half_box.at[pl.ds(1, groups - 1)]
    pltpu.make_async_copy(others, others, v2.at[0]).wait()
    value = mine[core, group]
    for d in range(1, groups):
        value = value + half_box[d]
    pltpu.make_async_copy(others, others, s2.at[0]).wait()
    full[core, group] = value * scale
    for d in range(1, groups):
        own = full.at[core, group]
        remote(own, own, s3.at[0], v3.at[0], peer(d)[1])
    advance(sum(WINDOW[:3]))
    pltpu.make_async_copy(others, others, v3.at[0]).wait()
    pltpu.make_async_copy(others, others, s3.at[0]).wait()
    exchange = remote(full.at[core], full.at[core], s4.at[0], v4.at[0], twin)
    advance(sum(WINDOW))
    exchange.wait()
    for c in range(2):
        for g in range(groups):
            first = (c * groups + g) * eight
            acc[first : first + eight, :] = full[c, g]
    turned_ref[...] = basis_from(acc[...], prior[...])

    left_hi, left_lo = split(turned_ref[...])
    left = jnp.concatenate([left_hi, left_lo], axis=0)
    a_group = 32
    per = rank // narrow
    band = width // wide
    to_core, to_chip, to_wide = {}, {}, {}

    def apply(j):
        def one(k, carry):
            hi, lo = split(
                jnp.concatenate(
                    [
                        flat[pl.ds((j * width + k * a_group + t) * skew, order), :]
                        for t in range(a_group)
                    ],
                    axis=1,
                )
            )
            both = jnp.dot(left, hi, preferred_element_type=F32)
            value = both[:rank] + (both[rank:] + jnp.dot(left_hi, lo, preferred_element_type=F32))
            for h in range(narrow):
                for t in range(a_group):
                    second[j, h % 2, h // 2, k * a_group + t] = value[
                        h * per : (h + 1) * per, t * cells : (t + 1) * cells
                    ]
            return carry

        lax.fori_loop(0, width // a_group, one, 0)
        to_core[j] = remote(second.at[j, 1 - core], core_box.at[j], sc.at[j], rc.at[j], twin)

    def merge(j):
        to_core[j].wait_recv()
        for h in range(1, chips):
            other = lax.rem(chip + h, chips)
            second[j, core, other] = second[j, core, other] + core_box[j, other]
            to_chip[j, h] = remote(
                second.at[j, core, other], chip_box.at[j, h], sy.at[j, h], ry.at[j, h],
                {"narrow": other * 2 + core},
            )

    def spread(j):
        value = second[j, core, chip] + core_box[j, chip]
        for h in range(1, chips):
            to_chip[j, h].wait_recv()
            value = value + chip_box[j, h]
        second[j, core, chip] = value
        for d in range(1, wide):
            to = lax.rem(place + d, wide)
            to_wide[j, d] = remote(
                second.at[j, core, chip, pl.ds(to * band, band)], wide_box.at[j, place],
                sw.at[j], rw.at[j], {"wide": to},
            )
        wide_box[j, place] = second[j, core, chip, pl.ds(place * band, band)]

    c_group = 8

    def collect(j):
        arrived = wide_box.at[j, pl.ds(1, wide - 1)]
        pltpu.make_async_copy(arrived, arrived, rw.at[j]).wait()

        def some(k, carry):
            sums = [
                [
                    jnp.zeros((per, cells), F32) if j == 0 else total[k * c_group + c, b]
                    for b in range(band)
                ]
                for c in range(c_group)
            ]
            for w in range(wide):
                tiles = [wide_box[j, w, b] for b in range(band)]
                for c in range(c_group):
                    weight = three[k * c_group + c, w * depth + j]
                    for b in range(band):
                        sums[c][b] = sums[c][b] + tiles[b] * weight
            for c in range(c_group):
                for b in range(band):
                    total[k * c_group + c, b] = sums[c][b]
            return carry

        lax.fori_loop(0, three.shape[0] // c_group, some, 0)

    for j in range(depth + 4):
        if j < depth:
            advance((j + 1) * PARTS)
            apply(j)
            advance(AHEAD[j])
            merge(j)
        if 0 <= j - 2 < depth:
            spread(j - 2)
        if 0 <= j - 4 < depth:
            collect(j - 4)
    for copy in [*to_core.values(), *to_chip.values()]:
        copy.wait_send()
    for j in range(depth):
        sent = wide_box.at[j, pl.ds(1, wide - 1)]
        pltpu.make_async_copy(sent, sent, sw.at[j]).wait()
    ends = three.shape[0]
    result = out_ref.reshape(per * band * ends, cells)
    for c in range(ends):
        for b in range(band):
            result[pl.ds(b * ends + c, per, stride=band * ends), :] = total[c, b]


def fits(narrow, wide, shape, rank, width):
    order, rows_two, rows_three, cells = shape
    return (
        rank == narrow * SUBLANES
        and width % wide == 0
        and order % (narrow * wide * SUBLANES) == 0
        and rows_two * rows_three % 32 == 0
        and rows_two * rows_three >= 32 * DEPTH
        and rows_two % SUBLANES == 0
        and order * rows_two * rows_three * cells * 4 >= 64 << 20
    )


def fused(narrow, wide, table, prior, two, three):
    order, rows_two, depth, cells = table.shape
    rank, width, ends = prior.shape[1], two.shape[1], three.shape[1]
    rows = rows_two * depth
    tall = order // SUBLANES
    block = 32
    padded = block + SUBLANES
    groups = narrow // 2 * wide
    eight = order // (2 * groups)
    per, band, chips = rank // narrow, width // wide, narrow // 2
    lines_z = depth * width * (order + 1)
    slots = max(-(-lines_z // (tall * padded)), DEPTH * SUBLANES)
    share = order // PARTS
    dma = pltpu.SemaphoreType.DMA
    anywhere = pl.BlockSpec(memory_space=pl.ANY)
    local = pl.BlockSpec(memory_space=pltpu.VMEM)
    turned, core_out = pl.pallas_call(
        functools.partial(fused_kernel, narrow, wide, 1.0 / float(I2 * I3 * M)),
        in_specs=[anywhere] * 5,
        out_specs=[local, local],
        out_shape=[
            jax.ShapeDtypeStruct((rank, order), F32),
            jax.ShapeDtypeStruct((per, band, ends, cells), F32),
        ],
        scratch_shapes=[
            pltpu.VMEM((rank, order), F32),
            pltpu.VMEM((width, two.shape[0]), F32),
            pltpu.SMEM((ends, three.shape[0]), F32),
            pltpu.VMEM((slots, tall, padded, cells), F32),
            pltpu.VMEM((RING, share, rows_two, cells), F32),
            pltpu.VMEM((order, order), F32),
            pltpu.VMEM((order, order), F32),
            pltpu.VMEM((2, groups, eight, order), F32),
            pltpu.VMEM((groups, eight, order), F32),
            pltpu.VMEM((2, groups, eight, order), F32),
            pltpu.VMEM((depth, 2, chips, width, per, cells), F32),
            pltpu.VMEM((depth, chips, width, per, cells), F32),
            pltpu.VMEM((depth, chips, width, per, cells), F32),
            pltpu.VMEM((depth, wide, band, per, cells), F32),
            pltpu.VMEM((ends, band, per, cells), F32),
            dma((3,)), dma((DEPTH, SUBLANES)), dma((RING,)),
            *[dma((1,))] * 8,
            dma((depth,)), dma((depth,)),
            dma((depth, chips)), dma((depth, chips)),
            dma((depth,)), dma((depth,)),
        ],
        compiler_params=pltpu.CompilerParams(
            vmem_limit_bytes=60 << 20, collective_id=3, has_side_effects=True
        ),
    )(table.reshape(tall, SUBLANES, rows, cells), table, prior.T, two.T, three.T)
    return core_out, turned.T


def per_device(narrow, wide, table, prior_one, factor_two, factor_three):
    order, rows_two, rows_three, cells = table.shape
    if fits(narrow, wide, table.shape, prior_one.shape[1], factor_two.shape[1]):
        return fused(narrow, wide, table, prior_one, factor_two, factor_three)
    flat = table.reshape(order, rows_two * rows_three, cells)
    turned = basis_of(narrow, wide, gram_of(flat), prior_one)
    at = lax.axis_index("narrow")
    two = lax.dynamic_slice_in_dim(factor_two, at * rows_two, rows_two, 0).T
    spread = project(narrow, wide, turned, two, flat, rows_three)
    three = factor_three.reshape(wide, rows_three, factor_three.shape[1])
    core_out = jnp.einsum("wrbjm,wjc->rbcm", spread, three, precision=HIGH)
    return core_out, turned.T


def solution(mesh):
    return jax.shard_map(
        functools.partial(per_device, mesh.shape["narrow"], mesh.shape["wide"]),
        mesh=mesh,
        in_specs=(P(None, "narrow", "wide", None), P(), P(), P()),
        out_specs=(P("narrow", "wide", None, None), P()),
        check_vma=False,
    )
```

```python
import functools

import jax
import jax.numpy as jnp
from jax import lax
from jax.experimental import pallas as pl
from jax.experimental.pallas import tpu as pltpu
from jax.sharding import PartitionSpec as P

I2 = 256
I3 = 64
M = 128
SUB = 2
BATCH = 8

F32 = jnp.float32
BF16 = jnp.bfloat16
HIGH = lax.Precision.HIGHEST
NT = (((1,), (1,)), ((), ()))
TN = (((0,), (0,)), ((), ()))
MESH = pl.DeviceIdType.MESH


def split(x):
    hi = x.astype(BF16)
    return hi, (x - hi.astype(F32)).astype(BF16)


def gather_rows(ref, first, group):
    block = jnp.swapaxes(ref[:, pl.ds(pl.multiple_of(first, group), group), :], 0, 1)
    return jnp.concatenate([block[t] for t in range(group)], axis=1)


SUBLANES = 8
DEPTH = 3


def gram_kernel(block, group, table_ref, gram_ref, buf, acc, cross, sems):
    tall, lines, rows, cells = table_ref.shape
    padded = buf.shape[3]
    steps = rows // block
    acc[...] = jnp.zeros_like(acc)
    cross[...] = jnp.zeros_like(cross)

    def fetch(i, slot):
        first = pl.multiple_of(i * block, block)
        return [
            pltpu.make_async_copy(
                table_ref.at[:, s, pl.ds(first, block), :],
                buf.at[slot, s, :, pl.ds(s, block), :],
                sems.at[slot, s],
            )
            for s in range(lines)
        ]

    for i in range(min(DEPTH - 1, steps)):
        for copy in fetch(i, i):
            copy.start()
    flat = buf.reshape(DEPTH * lines * tall * padded, cells)
    stride = tall * padded + 1

    def body(i, carry):
        slot = lax.rem(i, DEPTH)
        ahead = i + DEPTH - 1

        @pl.when(ahead < steps)
        def _():
            for copy in fetch(ahead, lax.rem(ahead, DEPTH)):
                copy.start()

        for copy in fetch(i, slot):
            copy.wait()
        base = slot * (lines * tall * padded)

        def part(g, carry):
            columns = []
            for t in range(group):
                at = base + g * group + t
                columns.append(
                    jnp.concatenate(
                        [flat[pl.ds(at + q * padded, lines, stride=stride), :] for q in range(tall)],
                        axis=0,
                    )
                )
            hi, lo = split(jnp.concatenate(columns, axis=1))
            acc[...] += lax.dot_general(hi, hi, NT, preferred_element_type=F32)
            cross[...] += lax.dot_general(hi, lo, NT, preferred_element_type=F32)
            return carry

        return lax.fori_loop(0, block // group, part, carry)

    lax.fori_loop(0, steps, body, 0)
    gram_ref[...] = acc[...] + (cross[...] + cross[...].T)


def gram_of(flat):
    order, rows, cells = flat.shape
    block = min(32, rows)
    tall = order // SUBLANES
    return pl.pallas_call(
        functools.partial(gram_kernel, block, min(16, block)),
        in_specs=[pl.BlockSpec(memory_space=pl.ANY)],
        out_specs=pl.BlockSpec(memory_space=pltpu.VMEM),
        out_shape=jax.ShapeDtypeStruct((order, order), F32),
        scratch_shapes=[
            pltpu.VMEM((DEPTH, SUBLANES, tall, block + SUBLANES, cells), F32),
            pltpu.VMEM((order, order), F32),
            pltpu.VMEM((order, order), F32),
            pltpu.SemaphoreType.DMA((DEPTH, SUBLANES)),
        ],
        compiler_params=pltpu.CompilerParams(vmem_limit_bytes=48 << 20),
    )(flat.reshape(tall, SUBLANES, rows, cells))


def greet(narrow, wide, at, place):
    barrier = pltpu.get_barrier_semaphore()
    for d in range(1, narrow):
        pl.semaphore_signal(
            barrier, inc=1, device_id={"narrow": lax.rem(at + d, narrow)}, device_id_type=MESH
        )
    for d in range(1, wide):
        pl.semaphore_signal(
            barrier, inc=1, device_id={"wide": lax.rem(place + d, wide)}, device_id_type=MESH
        )


def send(src, dst, send_sem, recv_sem, axis, to):
    copy = pltpu.make_async_remote_copy(
        src_ref=src,
        dst_ref=dst,
        send_sem=send_sem,
        recv_sem=recv_sem,
        device_id={axis: to},
        device_id_type=MESH,
    )
    copy.start()
    return copy


def finish(copies):
    for copy in copies:
        copy.wait()


def basis_from(gram, prior):
    basis = prior.T
    rank = basis.shape[1]
    row = lax.broadcasted_iota(jnp.int32, (rank, 1), 0)
    lane = lax.broadcasted_iota(jnp.int32, (rank, rank), 1)
    unit = jnp.where(lane == lax.broadcasted_iota(jnp.int32, (rank, rank), 0), 1.0, 0.0)
    for _ in range(SUB):
        q = jnp.dot(gram, basis, precision=HIGH, preferred_element_type=F32)
        s = lax.dot_general(q, q, TN, precision=HIGH, preferred_element_type=F32)
        pair = jnp.concatenate([s, unit], axis=1)
        root = jnp.ones(pair.shape, F32)
        for k in range(0, rank, BATCH):
            wide = [jnp.broadcast_to(pair[:, k + i : k + i + 1], pair.shape) for i in range(BATCH)]
            for i in range(BATCH):
                pivot = wide[i][k + i : k + i + 1, :]
                back = 1.0 / pivot
                root = jnp.where(row == k + i, pivot, root)
                below = jnp.where(row > k + i, wide[i], 0.0)
                for t in range(i + 1, BATCH):
                    wide[t] = wide[t] - below * (wide[t][k + i : k + i + 1, :] * back)
                pair = pair - below * (pair[k + i : k + i + 1, :] * back)
        inverse = pair[:, rank:] * lax.rsqrt(root[:, :rank])
        basis = lax.dot_general(q, inverse, NT, precision=HIGH, preferred_element_type=F32)
    return basis.T


def basis_kernel(
    narrow, wide, scale, part_ref, prior_ref, turned_ref,
    box_n, mine, box_w, full, square, sn, rn, sw, rw, tw, vw, tn, vn,
):
    at, place = lax.axis_index("narrow"), lax.axis_index("wide")
    greet(narrow, wide, at, place)
    pl.semaphore_wait(pltpu.get_barrier_semaphore(), narrow + wide - 2)
    copies = []
    for d in range(1, narrow):
        to = lax.rem(at + d, narrow)
        copies.append(send(part_ref.at[to], box_n.at[d], sn.at[d], rn.at[d], "narrow", to))
    finish(copies)
    value = part_ref[at]
    for d in range(1, narrow):
        value = value + box_n[d]
    mine[...] = value
    copies = []
    for d in range(1, wide):
        to = lax.rem(place + d, wide)
        copies.append(send(mine.at[to], box_w.at[d], sw.at[d], rw.at[d], "wide", to))
    finish(copies)
    value = mine[place]
    for d in range(1, wide):
        value = value + box_w[d]
    full[at, place] = value * scale
    copies = []
    for d in range(1, wide):
        to = lax.rem(place + d, wide)
        own = full.at[at, place]
        copies.append(send(own, own, tw.at[d], vw.at[d], "wide", to))
    finish(copies)
    copies = []
    for d in range(1, narrow):
        to = lax.rem(at + d, narrow)
        own = full.at[at]
        copies.append(send(own, own, tn.at[d], vn.at[d], "narrow", to))
    finish(copies)
    small = full.shape[2]
    for i in range(narrow * wide):
        square[i * small : (i + 1) * small, :] = full[i // wide, i % wide]
    gram = square[...]
    turned_ref[...] = basis_from(gram, prior_ref[...])


def basis_of(narrow, wide, gram, prior):
    scale = 1.0 / float(I2 * I3 * M)
    order, rank = prior.shape
    small = order // (narrow * wide)
    dma = pltpu.SemaphoreType.DMA
    return pl.pallas_call(
        functools.partial(basis_kernel, narrow, wide, scale),
        in_specs=[pl.BlockSpec(memory_space=pltpu.VMEM)] * 2,
        out_specs=pl.BlockSpec(memory_space=pltpu.VMEM),
        out_shape=jax.ShapeDtypeStruct((rank, order), F32),
        scratch_shapes=[
            pltpu.VMEM((narrow, wide, small, order), F32),
            pltpu.VMEM((wide, small, order), F32),
            pltpu.VMEM((wide, small, order), F32),
            pltpu.VMEM((narrow, wide, small, order), F32),
            pltpu.VMEM((order, order), F32),
            dma((narrow,)), dma((narrow,)),
            dma((wide,)), dma((wide,)),
            dma((wide,)), dma((wide,)),
            dma((narrow,)), dma((narrow,)),
        ],
        compiler_params=pltpu.CompilerParams(collective_id=1, has_side_effects=True),
    )(gram.reshape(narrow, wide, small, order), prior.T)


def project_kernel(
    group, depth, narrow, wide, spread, turned_ref, two_ref, table_ref, out_ref,
    trunc, second, core_box, chip_box, wide_box, sc, rc, sy, ry, sw, rw,
):
    _, rows, cells = table_ref.shape
    rank = turned_ref.shape[0]
    total = trunc.shape[0] // rank
    tall = total // depth
    step = pl.program_id(0)
    at, place = lax.axis_index("narrow"), lax.axis_index("wide")

    @pl.when(step == 0)
    def _():
        greet(narrow, wide, at, place)

    left_hi, left_lo = split(turned_ref[...])
    left = jnp.concatenate([left_hi, left_lo], axis=0)

    def body(g, carry):
        hi, lo = split(gather_rows(table_ref, g * group, group))
        both = jnp.dot(left, hi, preferred_element_type=F32)
        value = both[:rank] + (both[rank:] + jnp.dot(left_hi, lo, preferred_element_type=F32))
        for t in range(group):
            spot = step * rows + g * group + t
            spot = lax.rem(spot, depth) * tall + spot // depth
            trunc[pl.ds(spot, rank, stride=total), :] = value[:, t * cells : (t + 1) * cells]
        return carry

    lax.fori_loop(0, rows // group, body, 0)

    @pl.when(step == pl.num_programs(0) - 1)
    def _():
        pl.semaphore_wait(pltpu.get_barrier_semaphore(), narrow + wide - 2)
        two_hi, two_lo = split(two_ref[...])
        two = jnp.concatenate([two_hi, two_lo], axis=0)
        width = two_ref.shape[0]
        per = rank // narrow
        slab = width * depth
        chips = narrow // 2
        chip, core = at // 2, lax.rem(at, 2)
        chunk, chunks = 1, per
        flat = second.reshape(rank * slab, cells)

        def compute(block, q):
            def one(k, carry):
                r = block * per + q * chunk + k
                parts = [
                    trunc[pl.ds(pl.multiple_of(r * total + j * tall, tall), tall), :]
                    for j in range(depth)
                ]
                hi, lo = split(jnp.concatenate(parts, axis=1))
                both = jnp.dot(two, hi, preferred_element_type=F32)
                value = both[:width] + (
                    both[width:] + jnp.dot(two_hi, lo, preferred_element_type=F32)
                )
                for j in range(depth):
                    flat[pl.ds(r * slab + j, width, stride=depth), :] = value[
                        :, j * cells : (j + 1) * cells
                    ]
                return carry

            lax.fori_loop(0, chunk, one, 0)

        def part(q):
            return pl.ds(q * chunk, chunk)

        def target(h):
            return lax.rem(chip + h, chips)

        to_core, to_chip, to_wide = {}, {}, []

        def start(h, q):
            other = target(h) * 2 + (1 - core)
            compute(other, q)
            to_core[h, q] = send(
                second.at[other, part(q)], core_box.at[h, part(q)],
                sc.at[h, q], rc.at[h, q], "narrow", chip * 2 + (1 - core),
            )
            compute(target(h) * 2 + core, q)

        def merge(h, q):
            to_core[h, q].wait_recv()
            block = target(h) * 2 + core
            second[block, part(q)] = second[block, part(q)] + core_box[h, part(q)]
            if h:
                to_chip[h, q] = send(
                    second.at[block, part(q)], chip_box.at[h - 1, part(q)],
                    sy.at[h, q], ry.at[h, q], "narrow", block,
                )

        pairs = [(h, q) for h in [*range(1, chips), 0] for q in range(chunks)]
        for i, pair in enumerate(pairs):
            start(*pair)
            if i:
                merge(*pairs[i - 1])
        merge(*pairs[-1])
        for q in range(chunks):
            value = second[at, part(q)]
            for h in range(1, chips):
                to_chip[h, q].wait_recv()
                value = value + chip_box[h - 1, part(q)]
            if not spread:
                out_ref[0, part(q)] = value
                continue
            second[at, part(q)] = value
            band = slab // wide
            for d in range(1, wide):
                to = lax.rem(place + d, wide)
                rows_to = pl.ds(pl.multiple_of(to * band, band), band)
                to_wide.append(
                    send(
                        second.at[at, part(q), rows_to], wide_box.at[place, part(q)],
                        sw.at[d, q], rw.at[d, q], "wide", to,
                    )
                )
            own = pl.ds(pl.multiple_of(place * band, band), band)
            out_ref[place, part(q)] = second[at, part(q), own]
        for copy in [*to_core.values(), *to_chip.values()]:
            copy.wait_send()
        finish(to_wide)
        if spread:
            for d in range(1, wide):
                source = lax.rem(place + d, wide)
                out_ref[source] = wide_box[source]


def project(narrow, wide, turned, two, flat, depth):
    order, rows, cells = flat.shape
    rank, width = turned.shape[0], two.shape[0]
    block = min(32, rows)
    per, slab, chips = rank // narrow, width * depth, narrow // 2
    spread = (slab // wide) % 8 == 0
    shape = (wide, per, slab // wide, cells) if spread else (1, per, slab, cells)
    chunks = per
    dma = pltpu.SemaphoreType.DMA
    out = pl.pallas_call(
        functools.partial(
            project_kernel, min(16, block), depth, narrow, wide, spread
        ),
        grid=(rows // block,),
        in_specs=[
            pl.BlockSpec(turned.shape, lambda i: (0, 0)),
            pl.BlockSpec(two.shape, lambda i: (0, 0)),
            pl.BlockSpec((order, block, cells), lambda i: (0, i, 0)),
        ],
        out_specs=pl.BlockSpec(shape, lambda i: (0, 0, 0, 0)),
        out_shape=jax.ShapeDtypeStruct(shape, F32),
        scratch_shapes=[
            pltpu.VMEM((rank * rows, cells), F32),
            pltpu.VMEM((narrow, per, slab, cells), F32),
            pltpu.VMEM((chips, per, slab, cells), F32),
            pltpu.VMEM((max(chips - 1, 1), per, slab, cells), F32),
            pltpu.VMEM(shape, F32),
            dma((chips, chunks)), dma((chips, chunks)),
            dma((chips, chunks)), dma((chips, chunks)),
            dma((wide, chunks)), dma((wide, chunks)),
        ],
        compiler_params=pltpu.CompilerParams(
            vmem_limit_bytes=56 << 20, collective_id=2, has_side_effects=True
        ),
    )(turned, two, flat)
    if not spread:
        out = out.reshape(per, wide, slab // wide, cells)
        out = lax.all_to_all(out, "wide", split_axis=1, concat_axis=1, tiled=True)
        out = out.transpose(1, 0, 2, 3)
    return out.reshape(wide, per, width // wide, depth, cells)


RING = 6
PARTS = 4
WINDOW = (2, 7, 7, 2)
AHEAD = (18, 18, 18, 20, 20, 21, 22, 23, 24, 25, 26, 28, 29, 31, 32, 32)


def fused_kernel(
    narrow, wide, scale,
    table_ref, view_ref, prior_hbm, two_hbm, three_hbm, turned_ref, total,
    prior, wholetwo, three, main, ring, acc, cross, mine, half_box, full, second,
    core_box, chip_box, wide_box,
    small_sem, gram_sem, ring_sem, s1, v1, s2, v2, s3, v3, s4, v4, sc, rc, sy, ry, sw, rw,
):
    tall, lines, rows, cells = table_ref.shape
    order, rows_two, depth, _ = view_ref.shape
    rank, width = prior_hbm.shape[0], two_hbm.shape[0]
    slots, _, padded, _ = main.shape
    block = padded - lines
    steps = rows // block
    at, place = lax.axis_index("narrow"), lax.axis_index("wide")
    chips = narrow // 2
    chip, core = at // 2, lax.rem(at, 2)
    groups = chips * wide
    group = chip * wide + place
    twin = {"narrow": chip * 2 + (1 - core)}

    def peer(d):
        to = lax.rem(group + d, groups)
        return to, {"narrow": (to // wide) * 2 + core, "wide": lax.rem(to, wide)}

    barrier = pltpu.get_barrier_semaphore()
    pl.semaphore_signal(barrier, inc=1, device_id=twin, device_id_type=MESH)
    for d in range(1, groups):
        pl.semaphore_signal(barrier, inc=1, device_id=peer(d)[1], device_id_type=MESH)

    small = [
        pltpu.make_async_copy(prior_hbm, prior, small_sem.at[0]),
        pltpu.make_async_copy(two_hbm, wholetwo, small_sem.at[1]),
        pltpu.make_async_copy(three_hbm, three, small_sem.at[2]),
    ]

    first_slot = slots - DEPTH * lines

    def fetch(i, slot):
        first = pl.multiple_of(i * block, block)
        return [
            pltpu.make_async_copy(
                table_ref.at[:, s, pl.ds(first, block), :],
                main.at[first_slot + slot * lines + s, :, pl.ds(s, block), :],
                gram_sem.at[slot, s],
            )
            for s in range(lines)
        ]

    share = order // PARTS
    pieces = depth * PARTS

    def piece(i, slot):
        first = pl.multiple_of(lax.rem(i, PARTS) * share, share)
        return pltpu.make_async_copy(
            view_ref.at[pl.ds(first, share), :, i // PARTS, :], ring.at[slot], ring_sem.at[slot]
        )

    for i in range(DEPTH - 1):
        for copy in fetch(i, i):
            copy.start()
    for copy in small:
        copy.start()
    acc[...] = jnp.zeros_like(acc)
    cross[...] = jnp.zeros_like(cross)
    flat = main.reshape(slots * tall * padded, cells)
    gather = tall * padded + 1
    lane_group = 16

    def gram_step(i, carry):
        slot = lax.rem(i, DEPTH)
        ahead = i + DEPTH - 1

        @pl.when(ahead < steps)
        def _():
            for copy in fetch(ahead, lax.rem(ahead, DEPTH)):
                copy.start()

        @pl.when(i == steps - 2)
        def _():
            for k in range(RING):
                piece(k, k).start()

        for copy in fetch(i, slot):
            copy.wait()
        base = (first_slot + slot * lines) * (tall * padded)

        def part(g, carry):
            columns = []
            for t in range(lane_group):
                spot = base + g * lane_group + t
                columns.append(
                    jnp.concatenate(
                        [flat[pl.ds(spot + q * padded, lines, stride=gather), :] for q in range(tall)],
                        axis=0,
                    )
                )
            hi, lo = split(jnp.concatenate(columns, axis=1))
            acc[...] += lax.dot_general(hi, hi, NT, preferred_element_type=F32)
            cross[...] += lax.dot_general(hi, lo, NT, preferred_element_type=F32)
            return carry

        return lax.fori_loop(0, block // lane_group, part, carry)

    lax.fori_loop(0, steps, gram_step, 0)
    for copy in small:
        copy.wait()

    narrowed = jnp.zeros((width, rows_two), F32)
    for d in range(narrow):
        narrowed = jnp.where(at == d, wholetwo[:, d * rows_two : (d + 1) * rows_two], narrowed)
    two_hi, two_lo = split(narrowed)
    two = jnp.concatenate([two_hi, two_lo], axis=0)
    skew = order + 1
    z_group = 64

    def reduce_piece(i, carry):
        slot = lax.rem(i, RING)
        piece(i, slot).wait()
        base = (i // PARTS) * (width * skew) + lax.rem(i, PARTS) * share

        def one(k, carry):
            hi, lo = split(
                jnp.concatenate([ring[slot, k * z_group + t] for t in range(z_group)], axis=1)
            )
            both = jnp.dot(two, hi, preferred_element_type=F32)
            value = both[:width] + (both[width:] + jnp.dot(two_hi, lo, preferred_element_type=F32))
            for t in range(z_group):
                flat[pl.ds(base + k * z_group + t, width, stride=skew), :] = value[
                    :, t * cells : (t + 1) * cells
                ]
            return carry

        lax.fori_loop(0, share // z_group, one, 0)

        @pl.when(i + RING < pieces)
        def _():
            piece(i + RING, slot).start()

        return carry

    state = [0]

    def advance(to):
        to = min(to, pieces)
        if to > state[0]:
            lax.fori_loop(state[0], to, reduce_piece, 0)
            state[0] = to

    def remote(src, dst, send_sem, recv_sem, to):
        copy = pltpu.make_async_remote_copy(
            src_ref=src, dst_ref=dst, send_sem=send_sem, recv_sem=recv_sem,
            device_id=to, device_id_type=MESH,
        )
        copy.start()
        return copy

    part = acc[...] + (cross[...] + cross[...].T)
    eight = order // (2 * groups)
    for c in range(2):
        for g in range(groups):
            first = (c * groups + g) * eight
            mine[c, g] = part[first : first + eight]
    pl.semaphore_wait(barrier, groups)
    exchange = remote(mine.at[1 - core], full.at[1 - core], s1.at[0], v1.at[0], twin)
    advance(WINDOW[0])
    exchange.wait()
    mine[core] = mine[core] + full[core]
    for d in range(1, groups):
        to, where = peer(d)
        remote(mine.at[core, to], half_box.at[d], s2.at[0], v2.at[0], where)
    advance(sum(WINDOW[:2]))
    others = half_box.at[pl.ds(1, groups - 1)]
    pltpu.make_async_copy(others, others, v2.at[0]).wait()
    value = mine[core, group]
    for d in range(1, groups):
        value = value + half_box[d]
    pltpu.make_async_copy(others, others, s2.at[0]).wait()
    full[core, group] = value * scale
    for d in range(1, groups):
        own = full.at[core, group]
        remote(own, own, s3.at[0], v3.at[0], peer(d)[1])
    advance(sum(WINDOW[:3]))
    pltpu.make_async_copy(others, others, v3.at[0]).wait()
    pltpu.make_async_copy(others, others, s3.at[0]).wait()
    exchange = remote(full.at[core], full.at[core], s4.at[0], v4.at[0], twin)
    advance(sum(WINDOW))
    exchange.wait()
    for c in range(2):
        for g in range(groups):
            first = (c * groups + g) * eight
            acc[first : first + eight, :] = full[c, g]
    turned_ref[...] = basis_from(acc[...], prior[...])

    left_hi, left_lo = split(turned_ref[...])
    left = jnp.concatenate([left_hi, left_lo], axis=0)
    per, band = rank // narrow, width // wide
    runs = wide // 2
    own, side = place // 2, lax.rem(place, 2)
    to_core, to_chip = {}, {}

    def apply(j, x):
        columns = [(i * 2 + x) * band + t for i in range(runs) for t in range(band)]
        hi, lo = split(
            jnp.concatenate([flat[pl.ds((j * width + b) * skew, order), :] for b in columns], axis=1)
        )
        both = jnp.dot(left, hi, preferred_element_type=F32)
        value = both[:rank] + (both[rank:] + jnp.dot(left_hi, lo, preferred_element_type=F32))
        for h in range(narrow):
            for t in range(len(columns)):
                second[j, x, h % 2, h // 2, t] = value[
                    h * per : (h + 1) * per, t * cells : (t + 1) * cells
                ]
        to_core[j, x] = remote(
            second.at[j, x, 1 - core], core_box.at[j, x], sc.at[j, x], rc.at[j, x], twin
        )

    def merge(j, x):
        to_core[j, x].wait_recv()
        for h in range(1, chips):
            other = lax.rem(chip + h, chips)
            second[j, x, core, other] = second[j, x, core, other] + core_box[j, x, other]
            to_chip[j, x, h] = remote(
                second.at[j, x, core, other], chip_box.at[j, x, h], sy.at[j, x, h], ry.at[j, x, h],
                {"narrow": other * 2 + core},
            )

    def spread(j, x):
        value = second[j, x, core, chip] + core_box[j, x, chip]
        for h in range(1, chips):
            to_chip[j, x, h].wait_recv()
            value = value + chip_box[j, x, h]
        second[j, x, core, chip] = value

        def deliver(i):
            remote(
                second.at[j, x, core, chip, pl.ds(i * band, band)], wide_box.at[j, place],
                sw.at[j], rw.at[j], {"wide": i * 2 + x},
            )

        for d in range(1, runs):
            deliver(lax.rem(own + d, runs))

        @pl.when(side != x)
        def _():
            deliver(own)

        @pl.when(side == x)
        def _():
            wide_box[j, place] = second[j, x, core, chip, pl.ds(own * band, band)]

    c_group = 8

    def collect(j):
        arrived = wide_box.at[j, pl.ds(1, wide - 1)]
        pltpu.make_async_copy(arrived, arrived, rw.at[j]).wait()

        def some(k, carry):
            sums = [
                [
                    jnp.zeros((per, cells), F32) if j == 0 else total[k * c_group + c, b]
                    for b in range(band)
                ]
                for c in range(c_group)
            ]
            for w in range(wide):
                tiles = [wide_box[j, w, b] for b in range(band)]
                for c in range(c_group):
                    weight = three[k * c_group + c, w * depth + j]
                    for b in range(band):
                        sums[c][b] = sums[c][b] + tiles[b] * weight
            for c in range(c_group):
                for b in range(band):
                    total[k * c_group + c, b] = sums[c][b]
            return carry

        lax.fori_loop(0, three.shape[0] // c_group, some, 0)

    units = [(j, x) for j in range(depth) for x in range(2)]
    for u in range(len(units) + 3):
        if u < len(units):
            advance((units[u][0] + 1) * PARTS)
            apply(*units[u])
            advance(AHEAD[u])
        if 1 <= u <= len(units):
            merge(*units[u - 1])
        if u >= 3:
            spread(*units[u - 3])
        if u >= 8 and u % 2 == 0:
            collect((u - 8) // 2)
    for j in range((len(units) - 4) // 2, depth):
        collect(j)
    for copy in [*to_core.values(), *to_chip.values()]:
        copy.wait_send()
    for j in range(depth):
        sent = wide_box.at[j, pl.ds(1, wide - 1)]
        pltpu.make_async_copy(sent, sent, sw.at[j]).wait()


def finish_kernel(total_ref, turned_ref, out_ref, basis_ref):
    ends, band, per, cells = total_ref.shape
    result = out_ref.reshape(per * band * ends, cells)
    for c in range(ends):
        for b in range(band):
            result[pl.ds(b * ends + c, per, stride=band * ends), :] = total_ref[c, b]
    basis_ref[...] = turned_ref[...]


def fits(narrow, wide, shape, rank, width):
    order, rows_two, rows_three, cells = shape
    return (
        rank == narrow * SUBLANES
        and width % wide == 0
        and wide % 2 == 0
        and order % (narrow * wide * SUBLANES) == 0
        and rows_two * rows_three % 32 == 0
        and rows_two * rows_three >= 32 * DEPTH
        and rows_two % SUBLANES == 0
        and order * rows_two * rows_three * cells * 4 >= 64 << 20
    )


def fused(narrow, wide, table, prior, two, three):
    order, rows_two, depth, cells = table.shape
    rank, width, ends = prior.shape[1], two.shape[1], three.shape[1]
    rows = rows_two * depth
    tall = order // SUBLANES
    block = 32
    padded = block + SUBLANES
    groups = narrow // 2 * wide
    eight = order // (2 * groups)
    per, band, chips = rank // narrow, width // wide, narrow // 2
    lines_z = depth * width * (order + 1)
    slots = max(-(-lines_z // (tall * padded)), DEPTH * SUBLANES)
    share, half = order // PARTS, width // 2
    dma = pltpu.SemaphoreType.DMA
    anywhere = pl.BlockSpec(memory_space=pl.ANY)
    local = pl.BlockSpec(memory_space=pltpu.VMEM)
    turned, total = pl.pallas_call(
        functools.partial(fused_kernel, narrow, wide, 1.0 / float(I2 * I3 * M)),
        in_specs=[anywhere] * 5,
        out_specs=[local, local],
        out_shape=[
            jax.ShapeDtypeStruct((rank, order), F32),
            jax.ShapeDtypeStruct((ends, band, per, cells), F32),
        ],
        scratch_shapes=[
            pltpu.VMEM((rank, order), F32),
            pltpu.VMEM((width, two.shape[0]), F32),
            pltpu.SMEM((ends, three.shape[0]), F32),
            pltpu.VMEM((slots, tall, padded, cells), F32),
            pltpu.VMEM((RING, share, rows_two, cells), F32),
            pltpu.VMEM((order, order), F32),
            pltpu.VMEM((order, order), F32),
            pltpu.VMEM((2, groups, eight, order), F32),
            pltpu.VMEM((groups, eight, order), F32),
            pltpu.VMEM((2, groups, eight, order), F32),
            pltpu.VMEM((depth, 2, 2, chips, half, per, cells), F32),
            pltpu.VMEM((depth, 2, chips, half, per, cells), F32),
            pltpu.VMEM((depth, 2, chips, half, per, cells), F32),
            pltpu.VMEM((depth, wide, band, per, cells), F32),
            dma((3,)), dma((DEPTH, SUBLANES)), dma((RING,)),
            *[dma((1,))] * 8,
            dma((depth, 2)), dma((depth, 2)),
            dma((depth, 2, chips)), dma((depth, 2, chips)),
            dma((depth,)), dma((depth,)),
        ],
        compiler_params=pltpu.CompilerParams(
            vmem_limit_bytes=60 << 20, collective_id=3, has_side_effects=True
        ),
    )(table.reshape(tall, SUBLANES, rows, cells), table, prior.T, two.T, three.T)
    core_out, turned = pl.pallas_call(
        finish_kernel,
        in_specs=[local, local],
        out_specs=[local, local],
        out_shape=[
            jax.ShapeDtypeStruct((per, band, ends, cells), F32),
            jax.ShapeDtypeStruct((rank, order), F32),
        ],
    )(total, turned)
    return core_out, turned.T


def per_device(narrow, wide, table, prior_one, factor_two, factor_three):
    order, rows_two, rows_three, cells = table.shape
    if fits(narrow, wide, table.shape, prior_one.shape[1], factor_two.shape[1]):
        return fused(narrow, wide, table, prior_one, factor_two, factor_three)
    flat = table.reshape(order, rows_two * rows_three, cells)
    turned = basis_of(narrow, wide, gram_of(flat), prior_one)
    at = lax.axis_index("narrow")
    two = lax.dynamic_slice_in_dim(factor_two, at * rows_two, rows_two, 0).T
    spread = project(narrow, wide, turned, two, flat, rows_three)
    three = factor_three.reshape(wide, rows_three, factor_three.shape[1])
    core_out = jnp.einsum("wrbjm,wjc->rbcm", spread, three, precision=HIGH)
    return core_out, turned.T


def solution(mesh):
    return jax.shard_map(
        functools.partial(per_device, mesh.shape["narrow"], mesh.shape["wide"]),
        mesh=mesh,
        in_specs=(P(None, "narrow", "wide", None), P(), P(), P()),
        out_specs=(P("narrow", "wide", None, None), P()),
        check_vma=False,
    )
```

```python
import functools

import jax
import jax.numpy as jnp
from jax import lax
from jax.experimental import pallas as pl
from jax.experimental.pallas import tpu as pltpu
from jax.sharding import PartitionSpec as P

I2 = 256
I3 = 64
M = 128
SUB = 2
BATCH = 8

F32 = jnp.float32
BF16 = jnp.bfloat16
HIGH = lax.Precision.HIGHEST
NT = (((1,), (1,)), ((), ()))
TN = (((0,), (0,)), ((), ()))
MESH = pl.DeviceIdType.MESH


def split(x):
    hi = x.astype(BF16)
    return hi, (x - hi.astype(F32)).astype(BF16)


def gather_rows(ref, first, group):
    block = jnp.swapaxes(ref[:, pl.ds(pl.multiple_of(first, group), group), :], 0, 1)
    return jnp.concatenate([block[t] for t in range(group)], axis=1)


SUBLANES = 8
DEPTH = 3


def gram_kernel(block, group, table_ref, gram_ref, buf, acc, cross, sems):
    tall, lines, rows, cells = table_ref.shape
    padded = buf.shape[3]
    steps = rows // block
    acc[...] = jnp.zeros_like(acc)
    cross[...] = jnp.zeros_like(cross)

    def fetch(i, slot):
        first = pl.multiple_of(i * block, block)
        return [
            pltpu.make_async_copy(
                table_ref.at[:, s, pl.ds(first, block), :],
                buf.at[slot, s, :, pl.ds(s, block), :],
                sems.at[slot, s],
            )
            for s in range(lines)
        ]

    for i in range(min(DEPTH - 1, steps)):
        for copy in fetch(i, i):
            copy.start()
    flat = buf.reshape(DEPTH * lines * tall * padded, cells)
    stride = tall * padded + 1

    def body(i, carry):
        slot = lax.rem(i, DEPTH)
        ahead = i + DEPTH - 1

        @pl.when(ahead < steps)
        def _():
            for copy in fetch(ahead, lax.rem(ahead, DEPTH)):
                copy.start()

        for copy in fetch(i, slot):
            copy.wait()
        base = slot * (lines * tall * padded)

        def part(g, carry):
            columns = []
            for t in range(group):
                at = base + g * group + t
                columns.append(
                    jnp.concatenate(
                        [flat[pl.ds(at + q * padded, lines, stride=stride), :] for q in range(tall)],
                        axis=0,
                    )
                )
            hi, lo = split(jnp.concatenate(columns, axis=1))
            acc[...] += lax.dot_general(hi, hi, NT, preferred_element_type=F32)
            cross[...] += lax.dot_general(hi, lo, NT, preferred_element_type=F32)
            return carry

        return lax.fori_loop(0, block // group, part, carry)

    lax.fori_loop(0, steps, body, 0)
    gram_ref[...] = acc[...] + (cross[...] + cross[...].T)


def gram_of(flat):
    order, rows, cells = flat.shape
    block = min(32, rows)
    tall = order // SUBLANES
    return pl.pallas_call(
        functools.partial(gram_kernel, block, min(16, block)),
        in_specs=[pl.BlockSpec(memory_space=pl.ANY)],
        out_specs=pl.BlockSpec(memory_space=pltpu.VMEM),
        out_shape=jax.ShapeDtypeStruct((order, order), F32),
        scratch_shapes=[
            pltpu.VMEM((DEPTH, SUBLANES, tall, block + SUBLANES, cells), F32),
            pltpu.VMEM((order, order), F32),
            pltpu.VMEM((order, order), F32),
            pltpu.SemaphoreType.DMA((DEPTH, SUBLANES)),
        ],
        compiler_params=pltpu.CompilerParams(vmem_limit_bytes=48 << 20),
    )(flat.reshape(tall, SUBLANES, rows, cells))


def greet(narrow, wide, at, place):
    barrier = pltpu.get_barrier_semaphore()
    for d in range(1, narrow):
        pl.semaphore_signal(
            barrier, inc=1, device_id={"narrow": lax.rem(at + d, narrow)}, device_id_type=MESH
        )
    for d in range(1, wide):
        pl.semaphore_signal(
            barrier, inc=1, device_id={"wide": lax.rem(place + d, wide)}, device_id_type=MESH
        )


def send(src, dst, send_sem, recv_sem, axis, to):
    copy = pltpu.make_async_remote_copy(
        src_ref=src,
        dst_ref=dst,
        send_sem=send_sem,
        recv_sem=recv_sem,
        device_id={axis: to},
        device_id_type=MESH,
    )
    copy.start()
    return copy


def finish(copies):
    for copy in copies:
        copy.wait()


def basis_from(gram, prior):
    basis = prior.T
    rank = basis.shape[1]
    row = lax.broadcasted_iota(jnp.int32, (rank, 1), 0)
    lane = lax.broadcasted_iota(jnp.int32, (rank, rank), 1)
    unit = jnp.where(lane == lax.broadcasted_iota(jnp.int32, (rank, rank), 0), 1.0, 0.0)
    for _ in range(SUB):
        q = jnp.dot(gram, basis, precision=HIGH, preferred_element_type=F32)
        s = lax.dot_general(q, q, TN, precision=HIGH, preferred_element_type=F32)
        pair = jnp.concatenate([s, unit], axis=1)
        root = jnp.ones(pair.shape, F32)
        for k in range(0, rank, BATCH):
            wide = [jnp.broadcast_to(pair[:, k + i : k + i + 1], pair.shape) for i in range(BATCH)]
            for i in range(BATCH):
                pivot = wide[i][k + i : k + i + 1, :]
                back = 1.0 / pivot
                root = jnp.where(row == k + i, pivot, root)
                below = jnp.where(row > k + i, wide[i], 0.0)
                for t in range(i + 1, BATCH):
                    wide[t] = wide[t] - below * (wide[t][k + i : k + i + 1, :] * back)
                pair = pair - below * (pair[k + i : k + i + 1, :] * back)
        inverse = pair[:, rank:] * lax.rsqrt(root[:, :rank])
        basis = lax.dot_general(q, inverse, NT, precision=HIGH, preferred_element_type=F32)
    return basis.T


def basis_kernel(
    narrow, wide, scale, part_ref, prior_ref, turned_ref,
    box_n, mine, box_w, full, square, sn, rn, sw, rw, tw, vw, tn, vn,
):
    at, place = lax.axis_index("narrow"), lax.axis_index("wide")
    greet(narrow, wide, at, place)
    pl.semaphore_wait(pltpu.get_barrier_semaphore(), narrow + wide - 2)
    copies = []
    for d in range(1, narrow):
        to = lax.rem(at + d, narrow)
        copies.append(send(part_ref.at[to], box_n.at[d], sn.at[d], rn.at[d], "narrow", to))
    finish(copies)
    value = part_ref[at]
    for d in range(1, narrow):
        value = value + box_n[d]
    mine[...] = value
    copies = []
    for d in range(1, wide):
        to = lax.rem(place + d, wide)
        copies.append(send(mine.at[to], box_w.at[d], sw.at[d], rw.at[d], "wide", to))
    finish(copies)
    value = mine[place]
    for d in range(1, wide):
        value = value + box_w[d]
    full[at, place] = value * scale
    copies = []
    for d in range(1, wide):
        to = lax.rem(place + d, wide)
        own = full.at[at, place]
        copies.append(send(own, own, tw.at[d], vw.at[d], "wide", to))
    finish(copies)
    copies = []
    for d in range(1, narrow):
        to = lax.rem(at + d, narrow)
        own = full.at[at]
        copies.append(send(own, own, tn.at[d], vn.at[d], "narrow", to))
    finish(copies)
    small = full.shape[2]
    for i in range(narrow * wide):
        square[i * small : (i + 1) * small, :] = full[i // wide, i % wide]
    gram = square[...]
    turned_ref[...] = basis_from(gram, prior_ref[...])


def basis_of(narrow, wide, gram, prior):
    scale = 1.0 / float(I2 * I3 * M)
    order, rank = prior.shape
    small = order // (narrow * wide)
    dma = pltpu.SemaphoreType.DMA
    return pl.pallas_call(
        functools.partial(basis_kernel, narrow, wide, scale),
        in_specs=[pl.BlockSpec(memory_space=pltpu.VMEM)] * 2,
        out_specs=pl.BlockSpec(memory_space=pltpu.VMEM),
        out_shape=jax.ShapeDtypeStruct((rank, order), F32),
        scratch_shapes=[
            pltpu.VMEM((narrow, wide, small, order), F32),
            pltpu.VMEM((wide, small, order), F32),
            pltpu.VMEM((wide, small, order), F32),
            pltpu.VMEM((narrow, wide, small, order), F32),
            pltpu.VMEM((order, order), F32),
            dma((narrow,)), dma((narrow,)),
            dma((wide,)), dma((wide,)),
            dma((wide,)), dma((wide,)),
            dma((narrow,)), dma((narrow,)),
        ],
        compiler_params=pltpu.CompilerParams(collective_id=1, has_side_effects=True),
    )(gram.reshape(narrow, wide, small, order), prior.T)


def project_kernel(
    group, depth, narrow, wide, spread, turned_ref, two_ref, table_ref, out_ref,
    trunc, second, core_box, chip_box, wide_box, sc, rc, sy, ry, sw, rw,
):
    _, rows, cells = table_ref.shape
    rank = turned_ref.shape[0]
    total = trunc.shape[0] // rank
    tall = total // depth
    step = pl.program_id(0)
    at, place = lax.axis_index("narrow"), lax.axis_index("wide")

    @pl.when(step == 0)
    def _():
        greet(narrow, wide, at, place)

    left_hi, left_lo = split(turned_ref[...])
    left = jnp.concatenate([left_hi, left_lo], axis=0)

    def body(g, carry):
        hi, lo = split(gather_rows(table_ref, g * group, group))
        both = jnp.dot(left, hi, preferred_element_type=F32)
        value = both[:rank] + (both[rank:] + jnp.dot(left_hi, lo, preferred_element_type=F32))
        for t in range(group):
            spot = step * rows + g * group + t
            spot = lax.rem(spot, depth) * tall + spot // depth
            trunc[pl.ds(spot, rank, stride=total), :] = value[:, t * cells : (t + 1) * cells]
        return carry

    lax.fori_loop(0, rows // group, body, 0)

    @pl.when(step == pl.num_programs(0) - 1)
    def _():
        pl.semaphore_wait(pltpu.get_barrier_semaphore(), narrow + wide - 2)
        two_hi, two_lo = split(two_ref[...])
        two = jnp.concatenate([two_hi, two_lo], axis=0)
        width = two_ref.shape[0]
        per = rank // narrow
        slab = width * depth
        chips = narrow // 2
        chip, core = at // 2, lax.rem(at, 2)
        chunk, chunks = 1, per
        flat = second.reshape(rank * slab, cells)

        def compute(block, q):
            def one(k, carry):
                r = block * per + q * chunk + k
                parts = [
                    trunc[pl.ds(pl.multiple_of(r * total + j * tall, tall), tall), :]
                    for j in range(depth)
                ]
                hi, lo = split(jnp.concatenate(parts, axis=1))
                both = jnp.dot(two, hi, preferred_element_type=F32)
                value = both[:width] + (
                    both[width:] + jnp.dot(two_hi, lo, preferred_element_type=F32)
                )
                for j in range(depth):
                    flat[pl.ds(r * slab + j, width, stride=depth), :] = value[
                        :, j * cells : (j + 1) * cells
                    ]
                return carry

            lax.fori_loop(0, chunk, one, 0)

        def part(q):
            return pl.ds(q * chunk, chunk)

        def target(h):
            return lax.rem(chip + h, chips)

        to_core, to_chip, to_wide = {}, {}, []

        def start(h, q):
            other = target(h) * 2 + (1 - core)
            compute(other, q)
            to_core[h, q] = send(
                second.at[other, part(q)], core_box.at[h, part(q)],
                sc.at[h, q], rc.at[h, q], "narrow", chip * 2 + (1 - core),
            )
            compute(target(h) * 2 + core, q)

        def merge(h, q):
            to_core[h, q].wait_recv()
            block = target(h) * 2 + core
            second[block, part(q)] = second[block, part(q)] + core_box[h, part(q)]
            if h:
                to_chip[h, q] = send(
                    second.at[block, part(q)], chip_box.at[h - 1, part(q)],
                    sy.at[h, q], ry.at[h, q], "narrow", block,
                )

        pairs = [(h, q) for h in [*range(1, chips), 0] for q in range(chunks)]
        for i, pair in enumerate(pairs):
            start(*pair)
            if i:
                merge(*pairs[i - 1])
        merge(*pairs[-1])
        for q in range(chunks):
            value = second[at, part(q)]
            for h in range(1, chips):
                to_chip[h, q].wait_recv()
                value = value + chip_box[h - 1, part(q)]
            if not spread:
                out_ref[0, part(q)] = value
                continue
            second[at, part(q)] = value
            band = slab // wide
            for d in range(1, wide):
                to = lax.rem(place + d, wide)
                rows_to = pl.ds(pl.multiple_of(to * band, band), band)
                to_wide.append(
                    send(
                        second.at[at, part(q), rows_to], wide_box.at[place, part(q)],
                        sw.at[d, q], rw.at[d, q], "wide", to,
                    )
                )
            own = pl.ds(pl.multiple_of(place * band, band), band)
            out_ref[place, part(q)] = second[at, part(q), own]
        for copy in [*to_core.values(), *to_chip.values()]:
            copy.wait_send()
        finish(to_wide)
        if spread:
            for d in range(1, wide):
                source = lax.rem(place + d, wide)
                out_ref[source] = wide_box[source]


def project(narrow, wide, turned, two, flat, depth):
    order, rows, cells = flat.shape
    rank, width = turned.shape[0], two.shape[0]
    block = min(32, rows)
    per, slab, chips = rank // narrow, width * depth, narrow // 2
    spread = (slab // wide) % 8 == 0
    shape = (wide, per, slab // wide, cells) if spread else (1, per, slab, cells)
    chunks = per
    dma = pltpu.SemaphoreType.DMA
    out = pl.pallas_call(
        functools.partial(
            project_kernel, min(16, block), depth, narrow, wide, spread
        ),
        grid=(rows // block,),
        in_specs=[
            pl.BlockSpec(turned.shape, lambda i: (0, 0)),
            pl.BlockSpec(two.shape, lambda i: (0, 0)),
            pl.BlockSpec((order, block, cells), lambda i: (0, i, 0)),
        ],
        out_specs=pl.BlockSpec(shape, lambda i: (0, 0, 0, 0)),
        out_shape=jax.ShapeDtypeStruct(shape, F32),
        scratch_shapes=[
            pltpu.VMEM((rank * rows, cells), F32),
            pltpu.VMEM((narrow, per, slab, cells), F32),
            pltpu.VMEM((chips, per, slab, cells), F32),
            pltpu.VMEM((max(chips - 1, 1), per, slab, cells), F32),
            pltpu.VMEM(shape, F32),
            dma((chips, chunks)), dma((chips, chunks)),
            dma((chips, chunks)), dma((chips, chunks)),
            dma((wide, chunks)), dma((wide, chunks)),
        ],
        compiler_params=pltpu.CompilerParams(
            vmem_limit_bytes=56 << 20, collective_id=2, has_side_effects=True
        ),
    )(turned, two, flat)
    if not spread:
        out = out.reshape(per, wide, slab // wide, cells)
        out = lax.all_to_all(out, "wide", split_axis=1, concat_axis=1, tiled=True)
        out = out.transpose(1, 0, 2, 3)
    return out.reshape(wide, per, width // wide, depth, cells)


RING = 6
PARTS = 4
WINDOW = (2, 7, 7, 2)
AHEAD = (18, 18, 18, 20, 20, 21, 22, 23, 24, 25, 26, 28, 29, 31, 32, 32)


def fused_kernel(
    narrow, wide, scale,
    table_ref, view_ref, prior_hbm, two_hbm, three_hbm, turned_ref, total,
    prior, wholetwo, three, main, ring, acc, cross, mine, half_box, full, second,
    core_box, chip_box, wide_box,
    small_sem, gram_sem, ring_sem, s1, v1, s2, v2, s3, v3, s4, v4, sc, rc, sy, ry, sw, rw,
):
    tall, lines, rows, cells = table_ref.shape
    order, rows_two, depth, _ = view_ref.shape
    rank, width = prior_hbm.shape[0], two_hbm.shape[0]
    slots, _, padded, _ = main.shape
    block = padded - lines
    steps = rows // block
    at, place = lax.axis_index("narrow"), lax.axis_index("wide")
    chips = narrow // 2
    chip, core = at // 2, lax.rem(at, 2)
    groups = chips * wide
    group = chip * wide + place
    twin = {"narrow": chip * 2 + (1 - core)}

    def peer(d):
        to = lax.rem(group + d, groups)
        return to, {"narrow": (to // wide) * 2 + core, "wide": lax.rem(to, wide)}

    barrier = pltpu.get_barrier_semaphore()
    pl.semaphore_signal(barrier, inc=1, device_id=twin, device_id_type=MESH)
    for d in range(1, groups):
        pl.semaphore_signal(barrier, inc=1, device_id=peer(d)[1], device_id_type=MESH)

    small = [
        pltpu.make_async_copy(prior_hbm, prior, small_sem.at[0]),
        pltpu.make_async_copy(two_hbm, wholetwo, small_sem.at[1]),
        pltpu.make_async_copy(three_hbm, three, small_sem.at[2]),
    ]

    first_slot = slots - DEPTH * lines

    def fetch(i, slot):
        first = pl.multiple_of(i * block, block)
        return [
            pltpu.make_async_copy(
                table_ref.at[:, s, pl.ds(first, block), :],
                main.at[first_slot + slot * lines + s, :, pl.ds(s, block), :],
                gram_sem.at[slot, s],
            )
            for s in range(lines)
        ]

    share = order // PARTS
    pieces = depth * PARTS

    def piece(i, slot):
        first = pl.multiple_of(lax.rem(i, PARTS) * share, share)
        return pltpu.make_async_copy(
            view_ref.at[pl.ds(first, share), :, i // PARTS, :], ring.at[slot], ring_sem.at[slot]
        )

    for i in range(DEPTH - 1):
        for copy in fetch(i, i):
            copy.start()
    for copy in small:
        copy.start()
    acc[...] = jnp.zeros_like(acc)
    cross[...] = jnp.zeros_like(cross)
    flat = main.reshape(slots * tall * padded, cells)
    gather = tall * padded + 1
    lane_group = 16

    def gram_step(i, carry):
        slot = lax.rem(i, DEPTH)
        ahead = i + DEPTH - 1

        @pl.when(ahead < steps)
        def _():
            for copy in fetch(ahead, lax.rem(ahead, DEPTH)):
                copy.start()

        @pl.when(i == steps - 2)
        def _():
            for k in range(RING):
                piece(k, k).start()

        for copy in fetch(i, slot):
            copy.wait()
        base = (first_slot + slot * lines) * (tall * padded)

        def part(g, carry):
            columns = []
            for t in range(lane_group):
                spot = base + g * lane_group + t
                columns.append(
                    jnp.concatenate(
                        [flat[pl.ds(spot + q * padded, lines, stride=gather), :] for q in range(tall)],
                        axis=0,
                    )
                )
            hi, lo = split(jnp.concatenate(columns, axis=1))
            acc[...] += lax.dot_general(hi, hi, NT, preferred_element_type=F32)
            cross[...] += lax.dot_general(hi, lo, NT, preferred_element_type=F32)
            return carry

        return lax.fori_loop(0, block // lane_group, part, carry)

    lax.fori_loop(0, steps, gram_step, 0)
    for copy in small:
        copy.wait()

    narrowed = jnp.zeros((width, rows_two), F32)
    for d in range(narrow):
        narrowed = jnp.where(at == d, wholetwo[:, d * rows_two : (d + 1) * rows_two], narrowed)
    two_hi, two_lo = split(narrowed)
    two = jnp.concatenate(
        [
            jnp.concatenate([two_hi, two_hi], axis=1),
            jnp.concatenate([two_lo, jnp.zeros_like(two_lo)], axis=1),
        ],
        axis=0,
    )
    skew = order + 1
    z_group = 64

    def reduce_piece(i, carry):
        slot = lax.rem(i, RING)
        piece(i, slot).wait()
        base = (i // PARTS) * (width * skew) + lax.rem(i, PARTS) * share

        def one(k, carry):
            hi, lo = split(
                jnp.concatenate([ring[slot, k * z_group + t] for t in range(z_group)], axis=1)
            )
            stacked = jnp.concatenate([hi, lo], axis=0)
            both = jnp.dot(two, stacked, preferred_element_type=F32)
            value = both[:width] + both[width:]
            for t in range(z_group):
                flat[pl.ds(base + k * z_group + t, width, stride=skew), :] = value[
                    :, t * cells : (t + 1) * cells
                ]
            return carry

        lax.fori_loop(0, share // z_group, one, 0)

        @pl.when(i + RING < pieces)
        def _():
            piece(i + RING, slot).start()

        return carry

    state = [0]

    def advance(to):
        to = min(to, pieces)
        if to > state[0]:
            lax.fori_loop(state[0], to, reduce_piece, 0)
            state[0] = to

    def remote(src, dst, send_sem, recv_sem, to):
        copy = pltpu.make_async_remote_copy(
            src_ref=src, dst_ref=dst, send_sem=send_sem, recv_sem=recv_sem,
            device_id=to, device_id_type=MESH,
        )
        copy.start()
        return copy

    part = acc[...] + (cross[...] + cross[...].T)
    eight = order // (2 * groups)
    for c in range(2):
        for g in range(groups):
            first = (c * groups + g) * eight
            mine[c, g] = part[first : first + eight]
    pl.semaphore_wait(barrier, groups)
    exchange = remote(mine.at[1 - core], full.at[1 - core], s1.at[0], v1.at[0], twin)
    advance(WINDOW[0])
    exchange.wait()
    mine[core] = mine[core] + full[core]
    for d in range(1, groups):
        to, where = peer(d)
        remote(mine.at[core, to], half_box.at[d], s2.at[0], v2.at[0], where)
    advance(sum(WINDOW[:2]))
    others = half_box.at[pl.ds(1, groups - 1)]
    pltpu.make_async_copy(others, others, v2.at[0]).wait()
    value = mine[core, group]
    for d in range(1, groups):
        value = value + half_box[d]
    pltpu.make_async_copy(others, others, s2.at[0]).wait()
    full[core, group] = value * scale
    for d in range(1, groups):
        own = full.at[core, group]
        remote(own, own, s3.at[0], v3.at[0], peer(d)[1])
    advance(sum(WINDOW[:3]))
    pltpu.make_async_copy(others, others, v3.at[0]).wait()
    pltpu.make_async_copy(others, others, s3.at[0]).wait()
    exchange = remote(full.at[core], full.at[core], s4.at[0], v4.at[0], twin)
    advance(sum(WINDOW))
    exchange.wait()
    for c in range(2):
        for g in range(groups):
            first = (c * groups + g) * eight
            acc[first : first + eight, :] = full[c, g]
    turned_ref[...] = basis_from(acc[...], prior[...])

    left_hi, left_lo = split(turned_ref[...])
    left = jnp.concatenate([left_hi, left_lo], axis=0)
    per, band = rank // narrow, width // wide
    runs = wide // 2
    own, side = place // 2, lax.rem(place, 2)
    to_core, to_chip = {}, {}

    def apply(j, x):
        columns = [(i * 2 + x) * band + t for i in range(runs) for t in range(band)]
        hi, lo = split(
            jnp.concatenate([flat[pl.ds((j * width + b) * skew, order), :] for b in columns], axis=1)
        )
        both = jnp.dot(left, hi, preferred_element_type=F32)
        value = both[:rank] + (both[rank:] + jnp.dot(left_hi, lo, preferred_element_type=F32))
        for h in range(narrow):
            for t in range(len(columns)):
                second[j, x, h % 2, h // 2, t] = value[
                    h * per : (h + 1) * per, t * cells : (t + 1) * cells
                ]
        to_core[j, x] = remote(
            second.at[j, x, 1 - core], core_box.at[j, x], sc.at[j, x], rc.at[j, x], twin
        )

    def merge(j, x):
        to_core[j, x].wait_recv()
        for h in range(1, chips):
            other = lax.rem(chip + h, chips)
            second[j, x, core, other] = second[j, x, core, other] + core_box[j, x, other]
            to_chip[j, x, h] = remote(
                second.at[j, x, core, other], chip_box.at[j, x, h], sy.at[j, x, h], ry.at[j, x, h],
                {"narrow": other * 2 + core},
            )

    def spread(j, x):
        value = second[j, x, core, chip] + core_box[j, x, chip]
        for h in range(1, chips):
            to_chip[j, x, h].wait_recv()
            value = value + chip_box[j, x, h]
        second[j, x, core, chip] = value

        def deliver(i):
            remote(
                second.at[j, x, core, chip, pl.ds(i * band, band)], wide_box.at[j, place],
                sw.at[j], rw.at[j], {"wide": i * 2 + x},
            )

        for d in range(1, runs):
            deliver(lax.rem(own + d, runs))

        @pl.when(side != x)
        def _():
            deliver(own)

        @pl.when(side == x)
        def _():
            wide_box[j, place] = second[j, x, core, chip, pl.ds(own * band, band)]

    c_group = 8

    def collect(j):
        arrived = wide_box.at[j, pl.ds(1, wide - 1)]
        pltpu.make_async_copy(arrived, arrived, rw.at[j]).wait()

        def some(k, carry):
            sums = [
                [
                    jnp.zeros((per, cells), F32) if j == 0 else total[k * c_group + c, b]
                    for b in range(band)
                ]
                for c in range(c_group)
            ]
            for w in range(wide):
                tiles = [wide_box[j, w, b] for b in range(band)]
                for c in range(c_group):
                    weight = three[k * c_group + c, w * depth + j]
                    for b in range(band):
                        sums[c][b] = sums[c][b] + tiles[b] * weight
            for c in range(c_group):
                for b in range(band):
                    total[k * c_group + c, b] = sums[c][b]
            return carry

        lax.fori_loop(0, three.shape[0] // c_group, some, 0)

    units = [(j, x) for j in range(depth) for x in range(2)]
    for u in range(len(units) + 3):
        if u < len(units):
            advance((units[u][0] + 1) * PARTS)
            apply(*units[u])
            advance(AHEAD[u])
        if 1 <= u <= len(units):
            merge(*units[u - 1])
        if u >= 3:
            spread(*units[u - 3])
        if u >= 8 and u % 2 == 0:
            collect((u - 8) // 2)
    for j in range((len(units) - 4) // 2, depth):
        collect(j)
    for copy in [*to_core.values(), *to_chip.values()]:
        copy.wait_send()
    for j in range(depth):
        sent = wide_box.at[j, pl.ds(1, wide - 1)]
        pltpu.make_async_copy(sent, sent, sw.at[j]).wait()


def finish_kernel(total_ref, turned_ref, out_ref, basis_ref):
    ends, _, per, cells = total_ref.shape
    result = out_ref.reshape(per * ends, cells)
    for c in range(ends):
        result[pl.ds(c, per, stride=ends), :] = total_ref[c, 0]
    basis_ref[...] = turned_ref[...]


def fits(narrow, wide, shape, rank, width):
    order, rows_two, rows_three, cells = shape
    return (
        rank == narrow * SUBLANES
        and width % wide == 0
        and wide % 2 == 0
        and order % (narrow * wide * SUBLANES) == 0
        and rows_two * rows_three % 32 == 0
        and rows_two * rows_three >= 32 * DEPTH
        and rows_two % SUBLANES == 0
        and order * rows_two * rows_three * cells * 4 >= 64 << 20
    )


def fused(narrow, wide, table, prior, two, three):
    order, rows_two, depth, cells = table.shape
    rank, width, ends = prior.shape[1], two.shape[1], three.shape[1]
    rows = rows_two * depth
    tall = order // SUBLANES
    block = 32
    padded = block + SUBLANES
    groups = narrow // 2 * wide
    eight = order // (2 * groups)
    per, band, chips = rank // narrow, width // wide, narrow // 2
    lines_z = depth * width * (order + 1)
    slots = max(-(-lines_z // (tall * padded)), DEPTH * SUBLANES)
    share, half = order // PARTS, width // 2
    dma = pltpu.SemaphoreType.DMA
    anywhere = pl.BlockSpec(memory_space=pl.ANY)
    local = pl.BlockSpec(memory_space=pltpu.VMEM)
    turned, total = pl.pallas_call(
        functools.partial(fused_kernel, narrow, wide, 1.0 / float(I2 * I3 * M)),
        in_specs=[anywhere] * 5,
        out_specs=[local, local],
        out_shape=[
            jax.ShapeDtypeStruct((rank, order), F32),
            jax.ShapeDtypeStruct((ends, band, per, cells), F32),
        ],
        scratch_shapes=[
            pltpu.VMEM((rank, order), F32),
            pltpu.VMEM((width, two.shape[0]), F32),
            pltpu.SMEM((ends, three.shape[0]), F32),
            pltpu.VMEM((slots, tall, padded, cells), F32),
            pltpu.VMEM((RING, share, rows_two, cells), F32),
            pltpu.VMEM((order, order), F32),
            pltpu.VMEM((order, order), F32),
            pltpu.VMEM((2, groups, eight, order), F32),
            pltpu.VMEM((groups, eight, order), F32),
            pltpu.VMEM((2, groups, eight, order), F32),
            pltpu.VMEM((depth, 2, 2, chips, half, per, cells), F32),
            pltpu.VMEM((depth, 2, chips, half, per, cells), F32),
            pltpu.VMEM((depth, 2, chips, half, per, cells), F32),
            pltpu.VMEM((depth, wide, band, per, cells), F32),
            dma((3,)), dma((DEPTH, SUBLANES)), dma((RING,)),
            *[dma((1,))] * 8,
            dma((depth, 2)), dma((depth, 2)),
            dma((depth, 2, chips)), dma((depth, 2, chips)),
            dma((depth,)), dma((depth,)),
        ],
        compiler_params=pltpu.CompilerParams(
            vmem_limit_bytes=60 << 20, collective_id=3, has_side_effects=True
        ),
    )(table.reshape(tall, SUBLANES, rows, cells), table, prior.T, two.T, three.T)
    core_out, turned = pl.pallas_call(
        finish_kernel,
        grid=(band,),
        in_specs=[
            pl.BlockSpec((ends, 1, per, cells), lambda i: (0, i, 0, 0)),
            pl.BlockSpec((rank, order), lambda i: (0, 0)),
        ],
        out_specs=[
            pl.BlockSpec((per, 1, ends, cells), lambda i: (0, i, 0, 0)),
            pl.BlockSpec((rank, order), lambda i: (0, 0)),
        ],
        out_shape=[
            jax.ShapeDtypeStruct((per, band, ends, cells), F32),
            jax.ShapeDtypeStruct((rank, order), F32),
        ],
    )(total, turned)
    return core_out, turned.T


def per_device(narrow, wide, table, prior_one, factor_two, factor_three):
    order, rows_two, rows_three, cells = table.shape
    if fits(narrow, wide, table.shape, prior_one.shape[1], factor_two.shape[1]):
        return fused(narrow, wide, table, prior_one, factor_two, factor_three)
    flat = table.reshape(order, rows_two * rows_three, cells)
    turned = basis_of(narrow, wide, gram_of(flat), prior_one)
    at = lax.axis_index("narrow")
    two = lax.dynamic_slice_in_dim(factor_two, at * rows_two, rows_two, 0).T
    spread = project(narrow, wide, turned, two, flat, rows_three)
    three = factor_three.reshape(wide, rows_three, factor_three.shape[1])
    core_out = jnp.einsum("wrbjm,wjc->rbcm", spread, three, precision=HIGH)
    return core_out, turned.T


def solution(mesh):
    return jax.shard_map(
        functools.partial(per_device, mesh.shape["narrow"], mesh.shape["wide"]),
        mesh=mesh,
        in_specs=(P(None, "narrow", "wide", None), P(), P(), P()),
        out_specs=(P("narrow", "wide", None, None), P()),
        check_vma=False,
    )
```

```python
import functools

import jax
import jax.numpy as jnp
from jax import lax
from jax.experimental import pallas as pl
from jax.experimental.pallas import tpu as pltpu
from jax.sharding import PartitionSpec as P

I2 = 256
I3 = 64
M = 128
SUB = 2
BATCH = 8

F32 = jnp.float32
BF16 = jnp.bfloat16
HIGH = lax.Precision.HIGHEST
NT = (((1,), (1,)), ((), ()))
TN = (((0,), (0,)), ((), ()))
MESH = pl.DeviceIdType.MESH


def split(x):
    hi = x.astype(BF16)
    return hi, (x - hi.astype(F32)).astype(BF16)


def gather_rows(ref, first, group):
    block = jnp.swapaxes(ref[:, pl.ds(pl.multiple_of(first, group), group), :], 0, 1)
    return jnp.concatenate([block[t] for t in range(group)], axis=1)


SUBLANES = 8
DEPTH = 3


def gram_kernel(block, group, table_ref, gram_ref, buf, acc, cross, sems):
    tall, lines, rows, cells = table_ref.shape
    padded = buf.shape[3]
    steps = rows // block
    acc[...] = jnp.zeros_like(acc)
    cross[...] = jnp.zeros_like(cross)

    def fetch(i, slot):
        first = pl.multiple_of(i * block, block)
        return [
            pltpu.make_async_copy(
                table_ref.at[:, s, pl.ds(first, block), :],
                buf.at[slot, s, :, pl.ds(s, block), :],
                sems.at[slot, s],
            )
            for s in range(lines)
        ]

    for i in range(min(DEPTH - 1, steps)):
        for copy in fetch(i, i):
            copy.start()
    flat = buf.reshape(DEPTH * lines * tall * padded, cells)
    stride = tall * padded + 1

    def body(i, carry):
        slot = lax.rem(i, DEPTH)
        ahead = i + DEPTH - 1

        @pl.when(ahead < steps)
        def _():
            for copy in fetch(ahead, lax.rem(ahead, DEPTH)):
                copy.start()

        for copy in fetch(i, slot):
            copy.wait()
        base = slot * (lines * tall * padded)

        def part(g, carry):
            columns = []
            for t in range(group):
                at = base + g * group + t
                columns.append(
                    jnp.concatenate(
                        [flat[pl.ds(at + q * padded, lines, stride=stride), :] for q in range(tall)],
                        axis=0,
                    )
                )
            hi, lo = split(jnp.concatenate(columns, axis=1))
            acc[...] += lax.dot_general(hi, hi, NT, preferred_element_type=F32)
            cross[...] += lax.dot_general(hi, lo, NT, preferred_element_type=F32)
            return carry

        return lax.fori_loop(0, block // group, part, carry)

    lax.fori_loop(0, steps, body, 0)
    gram_ref[...] = acc[...] + (cross[...] + cross[...].T)


def gram_of(flat):
    order, rows, cells = flat.shape
    block = min(32, rows)
    tall = order // SUBLANES
    return pl.pallas_call(
        functools.partial(gram_kernel, block, min(16, block)),
        in_specs=[pl.BlockSpec(memory_space=pl.ANY)],
        out_specs=pl.BlockSpec(memory_space=pltpu.VMEM),
        out_shape=jax.ShapeDtypeStruct((order, order), F32),
        scratch_shapes=[
            pltpu.VMEM((DEPTH, SUBLANES, tall, block + SUBLANES, cells), F32),
            pltpu.VMEM((order, order), F32),
            pltpu.VMEM((order, order), F32),
            pltpu.SemaphoreType.DMA((DEPTH, SUBLANES)),
        ],
        compiler_params=pltpu.CompilerParams(vmem_limit_bytes=48 << 20),
    )(flat.reshape(tall, SUBLANES, rows, cells))


def greet(narrow, wide, at, place):
    barrier = pltpu.get_barrier_semaphore()
    for d in range(1, narrow):
        pl.semaphore_signal(
            barrier, inc=1, device_id={"narrow": lax.rem(at + d, narrow)}, device_id_type=MESH
        )
    for d in range(1, wide):
        pl.semaphore_signal(
            barrier, inc=1, device_id={"wide": lax.rem(place + d, wide)}, device_id_type=MESH
        )


def send(src, dst, send_sem, recv_sem, axis, to):
    copy = pltpu.make_async_remote_copy(
        src_ref=src,
        dst_ref=dst,
        send_sem=send_sem,
        recv_sem=recv_sem,
        device_id={axis: to},
        device_id_type=MESH,
    )
    copy.start()
    return copy


def finish(copies):
    for copy in copies:
        copy.wait()


def basis_from(gram, prior):
    basis = prior.T
    rank = basis.shape[1]
    row = lax.broadcasted_iota(jnp.int32, (rank, 1), 0)
    lane = lax.broadcasted_iota(jnp.int32, (rank, rank), 1)
    unit = jnp.where(lane == lax.broadcasted_iota(jnp.int32, (rank, rank), 0), 1.0, 0.0)
    for _ in range(SUB):
        q = jnp.dot(gram, basis, precision=HIGH, preferred_element_type=F32)
        s = lax.dot_general(q, q, TN, precision=HIGH, preferred_element_type=F32)
        pair = jnp.concatenate([s, unit], axis=1)
        root = jnp.ones(pair.shape, F32)
        for k in range(0, rank, BATCH):
            wide = [jnp.broadcast_to(pair[:, k + i : k + i + 1], pair.shape) for i in range(BATCH)]
            for i in range(BATCH):
                pivot = wide[i][k + i : k + i + 1, :]
                back = 1.0 / pivot
                root = jnp.where(row == k + i, pivot, root)
                below = jnp.where(row > k + i, wide[i], 0.0)
                for t in range(i + 1, BATCH):
                    wide[t] = wide[t] - below * (wide[t][k + i : k + i + 1, :] * back)
                pair = pair - below * (pair[k + i : k + i + 1, :] * back)
        inverse = pair[:, rank:] * lax.rsqrt(root[:, :rank])
        basis = lax.dot_general(q, inverse, NT, precision=HIGH, preferred_element_type=F32)
    return basis.T


def basis_kernel(
    narrow, wide, scale, part_ref, prior_ref, turned_ref,
    box_n, mine, box_w, full, square, sn, rn, sw, rw, tw, vw, tn, vn,
):
    at, place = lax.axis_index("narrow"), lax.axis_index("wide")
    greet(narrow, wide, at, place)
    pl.semaphore_wait(pltpu.get_barrier_semaphore(), narrow + wide - 2)
    copies = []
    for d in range(1, narrow):
        to = lax.rem(at + d, narrow)
        copies.append(send(part_ref.at[to], box_n.at[d], sn.at[d], rn.at[d], "narrow", to))
    finish(copies)
    value = part_ref[at]
    for d in range(1, narrow):
        value = value + box_n[d]
    mine[...] = value
    copies = []
    for d in range(1, wide):
        to = lax.rem(place + d, wide)
        copies.append(send(mine.at[to], box_w.at[d], sw.at[d], rw.at[d], "wide", to))
    finish(copies)
    value = mine[place]
    for d in range(1, wide):
        value = value + box_w[d]
    full[at, place] = value * scale
    copies = []
    for d in range(1, wide):
        to = lax.rem(place + d, wide)
        own = full.at[at, place]
        copies.append(send(own, own, tw.at[d], vw.at[d], "wide", to))
    finish(copies)
    copies = []
    for d in range(1, narrow):
        to = lax.rem(at + d, narrow)
        own = full.at[at]
        copies.append(send(own, own, tn.at[d], vn.at[d], "narrow", to))
    finish(copies)
    small = full.shape[2]
    for i in range(narrow * wide):
        square[i * small : (i + 1) * small, :] = full[i // wide, i % wide]
    gram = square[...]
    turned_ref[...] = basis_from(gram, prior_ref[...])


def basis_of(narrow, wide, gram, prior):
    scale = 1.0 / float(I2 * I3 * M)
    order, rank = prior.shape
    small = order // (narrow * wide)
    dma = pltpu.SemaphoreType.DMA
    return pl.pallas_call(
        functools.partial(basis_kernel, narrow, wide, scale),
        in_specs=[pl.BlockSpec(memory_space=pltpu.VMEM)] * 2,
        out_specs=pl.BlockSpec(memory_space=pltpu.VMEM),
        out_shape=jax.ShapeDtypeStruct((rank, order), F32),
        scratch_shapes=[
            pltpu.VMEM((narrow, wide, small, order), F32),
            pltpu.VMEM((wide, small, order), F32),
            pltpu.VMEM((wide, small, order), F32),
            pltpu.VMEM((narrow, wide, small, order), F32),
            pltpu.VMEM((order, order), F32),
            dma((narrow,)), dma((narrow,)),
            dma((wide,)), dma((wide,)),
            dma((wide,)), dma((wide,)),
            dma((narrow,)), dma((narrow,)),
        ],
        compiler_params=pltpu.CompilerParams(collective_id=1, has_side_effects=True),
    )(gram.reshape(narrow, wide, small, order), prior.T)


def project_kernel(
    group, depth, narrow, wide, spread, turned_ref, two_ref, table_ref, out_ref,
    trunc, second, core_box, chip_box, wide_box, sc, rc, sy, ry, sw, rw,
):
    _, rows, cells = table_ref.shape
    rank = turned_ref.shape[0]
    total = trunc.shape[0] // rank
    tall = total // depth
    step = pl.program_id(0)
    at, place = lax.axis_index("narrow"), lax.axis_index("wide")

    @pl.when(step == 0)
    def _():
        greet(narrow, wide, at, place)

    left_hi, left_lo = split(turned_ref[...])
    left = jnp.concatenate([left_hi, left_lo], axis=0)

    def body(g, carry):
        hi, lo = split(gather_rows(table_ref, g * group, group))
        both = jnp.dot(left, hi, preferred_element_type=F32)
        value = both[:rank] + (both[rank:] + jnp.dot(left_hi, lo, preferred_element_type=F32))
        for t in range(group):
            spot = step * rows + g * group + t
            spot = lax.rem(spot, depth) * tall + spot // depth
            trunc[pl.ds(spot, rank, stride=total), :] = value[:, t * cells : (t + 1) * cells]
        return carry

    lax.fori_loop(0, rows // group, body, 0)

    @pl.when(step == pl.num_programs(0) - 1)
    def _():
        pl.semaphore_wait(pltpu.get_barrier_semaphore(), narrow + wide - 2)
        two_hi, two_lo = split(two_ref[...])
        two = jnp.concatenate([two_hi, two_lo], axis=0)
        width = two_ref.shape[0]
        per = rank // narrow
        slab = width * depth
        chips = narrow // 2
        chip, core = at // 2, lax.rem(at, 2)
        chunk, chunks = 1, per
        flat = second.reshape(rank * slab, cells)

        def compute(block, q):
            def one(k, carry):
                r = block * per + q * chunk + k
                parts = [
                    trunc[pl.ds(pl.multiple_of(r * total + j * tall, tall), tall), :]
                    for j in range(depth)
                ]
                hi, lo = split(jnp.concatenate(parts, axis=1))
                both = jnp.dot(two, hi, preferred_element_type=F32)
                value = both[:width] + (
                    both[width:] + jnp.dot(two_hi, lo, preferred_element_type=F32)
                )
                for j in range(depth):
                    flat[pl.ds(r * slab + j, width, stride=depth), :] = value[
                        :, j * cells : (j + 1) * cells
                    ]
                return carry

            lax.fori_loop(0, chunk, one, 0)

        def part(q):
            return pl.ds(q * chunk, chunk)

        def target(h):
            return lax.rem(chip + h, chips)

        to_core, to_chip, to_wide = {}, {}, []

        def start(h, q):
            other = target(h) * 2 + (1 - core)
            compute(other, q)
            to_core[h, q] = send(
                second.at[other, part(q)], core_box.at[h, part(q)],
                sc.at[h, q], rc.at[h, q], "narrow", chip * 2 + (1 - core),
            )
            compute(target(h) * 2 + core, q)

        def merge(h, q):
            to_core[h, q].wait_recv()
            block = target(h) * 2 + core
            second[block, part(q)] = second[block, part(q)] + core_box[h, part(q)]
            if h:
                to_chip[h, q] = send(
                    second.at[block, part(q)], chip_box.at[h - 1, part(q)],
                    sy.at[h, q], ry.at[h, q], "narrow", block,
                )

        pairs = [(h, q) for h in [*range(1, chips), 0] for q in range(chunks)]
        for i, pair in enumerate(pairs):
            start(*pair)
            if i:
                merge(*pairs[i - 1])
        merge(*pairs[-1])
        for q in range(chunks):
            value = second[at, part(q)]
            for h in range(1, chips):
                to_chip[h, q].wait_recv()
                value = value + chip_box[h - 1, part(q)]
            if not spread:
                out_ref[0, part(q)] = value
                continue
            second[at, part(q)] = value
            band = slab // wide
            for d in range(1, wide):
                to = lax.rem(place + d, wide)
                rows_to = pl.ds(pl.multiple_of(to * band, band), band)
                to_wide.append(
                    send(
                        second.at[at, part(q), rows_to], wide_box.at[place, part(q)],
                        sw.at[d, q], rw.at[d, q], "wide", to,
                    )
                )
            own = pl.ds(pl.multiple_of(place * band, band), band)
            out_ref[place, part(q)] = second[at, part(q), own]
        for copy in [*to_core.values(), *to_chip.values()]:
            copy.wait_send()
        finish(to_wide)
        if spread:
            for d in range(1, wide):
                source = lax.rem(place + d, wide)
                out_ref[source] = wide_box[source]


def project(narrow, wide, turned, two, flat, depth):
    order, rows, cells = flat.shape
    rank, width = turned.shape[0], two.shape[0]
    block = min(32, rows)
    per, slab, chips = rank // narrow, width * depth, narrow // 2
    spread = (slab // wide) % 8 == 0
    shape = (wide, per, slab // wide, cells) if spread else (1, per, slab, cells)
    chunks = per
    dma = pltpu.SemaphoreType.DMA
    out = pl.pallas_call(
        functools.partial(
            project_kernel, min(16, block), depth, narrow, wide, spread
        ),
        grid=(rows // block,),
        in_specs=[
            pl.BlockSpec(turned.shape, lambda i: (0, 0)),
            pl.BlockSpec(two.shape, lambda i: (0, 0)),
            pl.BlockSpec((order, block, cells), lambda i: (0, i, 0)),
        ],
        out_specs=pl.BlockSpec(shape, lambda i: (0, 0, 0, 0)),
        out_shape=jax.ShapeDtypeStruct(shape, F32),
        scratch_shapes=[
            pltpu.VMEM((rank * rows, cells), F32),
            pltpu.VMEM((narrow, per, slab, cells), F32),
            pltpu.VMEM((chips, per, slab, cells), F32),
            pltpu.VMEM((max(chips - 1, 1), per, slab, cells), F32),
            pltpu.VMEM(shape, F32),
            dma((chips, chunks)), dma((chips, chunks)),
            dma((chips, chunks)), dma((chips, chunks)),
            dma((wide, chunks)), dma((wide, chunks)),
        ],
        compiler_params=pltpu.CompilerParams(
            vmem_limit_bytes=56 << 20, collective_id=2, has_side_effects=True
        ),
    )(turned, two, flat)
    if not spread:
        out = out.reshape(per, wide, slab // wide, cells)
        out = lax.all_to_all(out, "wide", split_axis=1, concat_axis=1, tiled=True)
        out = out.transpose(1, 0, 2, 3)
    return out.reshape(wide, per, width // wide, depth, cells)


RING = 6
PARTS = 4
WINDOW = (2, 7, 7, 2)
AHEAD = (18, 18, 18, 20, 20, 21, 22, 23, 24, 25, 26, 28, 29, 31, 32, 32)


def fused_kernel(
    narrow, wide, scale,
    table_ref, view_ref, prior_hbm, two_hbm, three_hbm, turned_ref, total,
    prior, wholetwo, three, main, ring, acc, cross, mine, half_box, full, second,
    core_box, chip_box, wide_box,
    small_sem, gram_sem, ring_sem, s1, v1, s2, v2, s3, v3, s4, v4, sc, rc, sy, ry, sw, rw,
):
    tall, lines, rows, cells = table_ref.shape
    order, rows_two, depth, _ = view_ref.shape
    rank, width = prior_hbm.shape[0], two_hbm.shape[0]
    slots, _, padded, _ = main.shape
    block = padded - lines
    steps = rows // block
    at, place = lax.axis_index("narrow"), lax.axis_index("wide")
    chips = narrow // 2
    chip, core = at // 2, lax.rem(at, 2)
    groups = chips * wide
    group = chip * wide + place
    twin = {"narrow": chip * 2 + (1 - core)}

    def peer(d):
        to = lax.rem(group + d, groups)
        return to, {"narrow": (to // wide) * 2 + core, "wide": lax.rem(to, wide)}

    barrier = pltpu.get_barrier_semaphore()
    pl.semaphore_signal(barrier, inc=1, device_id=twin, device_id_type=MESH)
    for d in range(1, groups):
        pl.semaphore_signal(barrier, inc=1, device_id=peer(d)[1], device_id_type=MESH)

    small = [
        pltpu.make_async_copy(prior_hbm, prior, small_sem.at[0]),
        pltpu.make_async_copy(two_hbm, wholetwo, small_sem.at[1]),
        pltpu.make_async_copy(three_hbm, three, small_sem.at[2]),
    ]

    first_slot = slots - DEPTH * lines

    def fetch(i, slot):
        first = pl.multiple_of(i * block, block)
        return [
            pltpu.make_async_copy(
                table_ref.at[:, s, pl.ds(first, block), :],
                main.at[first_slot + slot * lines + s, :, pl.ds(s, block), :],
                gram_sem.at[slot, s],
            )
            for s in range(lines)
        ]

    share = order // PARTS
    pieces = depth * PARTS

    def piece(i, slot):
        first = pl.multiple_of(lax.rem(i, PARTS) * share, share)
        return pltpu.make_async_copy(
            view_ref.at[pl.ds(first, share), :, i // PARTS, :], ring.at[slot], ring_sem.at[slot]
        )

    for i in range(DEPTH - 1):
        for copy in fetch(i, i):
            copy.start()
    for copy in small:
        copy.start()
    acc[...] = jnp.zeros_like(acc)
    cross[...] = jnp.zeros_like(cross)
    flat = main.reshape(slots * tall * padded, cells)
    gather = tall * padded + 1
    lane_group = 16

    def gram_step(i, carry):
        slot = lax.rem(i, DEPTH)
        ahead = i + DEPTH - 1

        @pl.when(ahead < steps)
        def _():
            for copy in fetch(ahead, lax.rem(ahead, DEPTH)):
                copy.start()

        @pl.when(i == steps - 2)
        def _():
            for k in range(RING):
                piece(k, k).start()

        for copy in fetch(i, slot):
            copy.wait()
        base = (first_slot + slot * lines) * (tall * padded)

        def part(g, carry):
            columns = []
            for t in range(lane_group):
                spot = base + g * lane_group + t
                columns.append(
                    jnp.concatenate(
                        [flat[pl.ds(spot + q * padded, lines, stride=gather), :] for q in range(tall)],
                        axis=0,
                    )
                )
            hi, lo = split(jnp.concatenate(columns, axis=1))
            acc[...] += lax.dot_general(hi, hi, NT, preferred_element_type=F32)
            cross[...] += lax.dot_general(hi, lo, NT, preferred_element_type=F32)
            return carry

        return lax.fori_loop(0, block // lane_group, part, carry)

    lax.fori_loop(0, steps, gram_step, 0)
    for copy in small:
        copy.wait()

    narrowed = jnp.zeros((width, rows_two), F32)
    for d in range(narrow):
        narrowed = jnp.where(at == d, wholetwo[:, d * rows_two : (d + 1) * rows_two], narrowed)
    two_hi, two_lo = split(narrowed)
    two = jnp.concatenate(
        [
            jnp.concatenate([two_hi, two_hi], axis=1),
            jnp.concatenate([two_lo, jnp.zeros_like(two_lo)], axis=1),
        ],
        axis=0,
    )
    skew = order + 1
    z_group = 64

    def reduce_piece(i, carry):
        slot = lax.rem(i, RING)
        piece(i, slot).wait()
        base = (i // PARTS) * (width * skew) + lax.rem(i, PARTS) * share

        def one(k, carry):
            hi, lo = split(
                jnp.concatenate([ring[slot, k * z_group + t] for t in range(z_group)], axis=1)
            )
            stacked = jnp.concatenate([hi, lo], axis=0)
            both = jnp.dot(two, stacked, preferred_element_type=F32)
            value = both[:width] + both[width:]
            for t in range(z_group):
                flat[pl.ds(base + k * z_group + t, width, stride=skew), :] = value[
                    :, t * cells : (t + 1) * cells
                ]
            return carry

        lax.fori_loop(0, share // z_group, one, 0)

        @pl.when(i + RING < pieces)
        def _():
            piece(i + RING, slot).start()

        return carry

    state = [0]

    def advance(to):
        to = min(to, pieces)
        if to > state[0]:
            lax.fori_loop(state[0], to, reduce_piece, 0)
            state[0] = to

    def remote(src, dst, send_sem, recv_sem, to):
        copy = pltpu.make_async_remote_copy(
            src_ref=src, dst_ref=dst, send_sem=send_sem, recv_sem=recv_sem,
            device_id=to, device_id_type=MESH,
        )
        copy.start()
        return copy

    part = acc[...] + (cross[...] + cross[...].T)
    eight = order // (2 * groups)
    for c in range(2):
        for g in range(groups):
            first = (c * groups + g) * eight
            mine[c, g] = part[first : first + eight]
    pl.semaphore_wait(barrier, groups)
    exchange = remote(mine.at[1 - core], full.at[1 - core], s1.at[0], v1.at[0], twin)
    advance(WINDOW[0])
    exchange.wait()
    mine[core] = mine[core] + full[core]
    for d in range(1, groups):
        to, where = peer(d)
        remote(mine.at[core, to], half_box.at[d], s2.at[0], v2.at[0], where)
    advance(sum(WINDOW[:2]))
    others = half_box.at[pl.ds(1, groups - 1)]
    pltpu.make_async_copy(others, others, v2.at[0]).wait()
    value = mine[core, group]
    for d in range(1, groups):
        value = value + half_box[d]
    pltpu.make_async_copy(others, others, s2.at[0]).wait()
    full[core, group] = value * scale
    for d in range(1, groups):
        own = full.at[core, group]
        remote(own, own, s3.at[0], v3.at[0], peer(d)[1])
    advance(sum(WINDOW[:3]))
    pltpu.make_async_copy(others, others, v3.at[0]).wait()
    pltpu.make_async_copy(others, others, s3.at[0]).wait()
    exchange = remote(full.at[core], full.at[core], s4.at[0], v4.at[0], twin)
    advance(sum(WINDOW))
    exchange.wait()
    for c in range(2):
        for g in range(groups):
            first = (c * groups + g) * eight
            acc[first : first + eight, :] = full[c, g]
    turned_ref[...] = basis_from(acc[...], prior[...])

    left_hi, left_lo = split(turned_ref[...])
    left = jnp.concatenate([left_hi, left_lo], axis=0)
    per, band = rank // narrow, width // wide
    runs = wide // 2
    own, side = place // 2, lax.rem(place, 2)
    to_core, to_chip = {}, {}

    def apply(j, x):
        columns = [(i * 2 + x) * band + t for i in range(runs) for t in range(band)]
        hi, lo = split(
            jnp.concatenate([flat[pl.ds((j * width + b) * skew, order), :] for b in columns], axis=1)
        )
        both = jnp.dot(left, hi, preferred_element_type=F32)
        value = both[:rank] + (both[rank:] + jnp.dot(left_hi, lo, preferred_element_type=F32))
        for h in range(narrow):
            for t in range(len(columns)):
                second[j, x, h % 2, h // 2, t] = value[
                    h * per : (h + 1) * per, t * cells : (t + 1) * cells
                ]
        to_core[j, x] = remote(
            second.at[j, x, 1 - core], core_box.at[j, x], sc.at[j, x], rc.at[j, x], twin
        )

    def merge(j, x):
        to_core[j, x].wait_recv()
        for h in range(1, chips):
            other = lax.rem(chip + h, chips)
            second[j, x, core, other] = second[j, x, core, other] + core_box[j, x, other]
            to_chip[j, x, h] = remote(
                second.at[j, x, core, other], chip_box.at[j, x, h], sy.at[j, x, h], ry.at[j, x, h],
                {"narrow": other * 2 + core},
            )

    def spread(j, x):
        value = second[j, x, core, chip] + core_box[j, x, chip]
        for h in range(1, chips):
            to_chip[j, x, h].wait_recv()
            value = value + chip_box[j, x, h]
        second[j, x, core, chip] = value

        def deliver(i):
            remote(
                second.at[j, x, core, chip, pl.ds(i * band, band)], wide_box.at[j, place],
                sw.at[j], rw.at[j], {"wide": i * 2 + x},
            )

        for d in range(1, runs):
            deliver(lax.rem(own + d, runs))

        @pl.when(side != x)
        def _():
            deliver(own)

        @pl.when(side == x)
        def _():
            wide_box[j, place] = second[j, x, core, chip, pl.ds(own * band, band)]

    c_group = 8

    def collect(j):
        arrived = wide_box.at[j, pl.ds(1, wide - 1)]
        pltpu.make_async_copy(arrived, arrived, rw.at[j]).wait()

        def some(k, carry):
            sums = [
                [
                    jnp.zeros((per, cells), F32) if j == 0 else total[k * c_group + c, b]
                    for b in range(band)
                ]
                for c in range(c_group)
            ]
            for w in range(wide):
                tiles = [wide_box[j, w, b] for b in range(band)]
                for c in range(c_group):
                    weight = three[k * c_group + c, w * depth + j]
                    for b in range(band):
                        sums[c][b] = sums[c][b] + tiles[b] * weight
            for c in range(c_group):
                for b in range(band):
                    total[k * c_group + c, b] = sums[c][b]
            return carry

        lax.fori_loop(0, three.shape[0] // c_group, some, 0)

    units = [(j, x) for j in range(depth) for x in range(2)]
    for u in range(len(units) + 3):
        if u < len(units):
            advance((units[u][0] + 1) * PARTS)
            apply(*units[u])
            advance(AHEAD[u])
        if 1 <= u <= len(units):
            merge(*units[u - 1])
        if u >= 3:
            spread(*units[u - 3])
        if u >= 8 and u % 2 == 0:
            collect((u - 8) // 2)
    for j in range((len(units) - 4) // 2, depth):
        collect(j)
    for copy in [*to_core.values(), *to_chip.values()]:
        copy.wait_send()
    for j in range(depth):
        sent = wide_box.at[j, pl.ds(1, wide - 1)]
        pltpu.make_async_copy(sent, sent, sw.at[j]).wait()


def finish_kernel(total_ref, turned_ref, out_ref, basis_ref):
    ends, band, per, cells = total_ref.shape
    result = out_ref.reshape(per * band * ends, cells)
    for c in range(ends):
        for b in range(band):
            result[pl.ds(b * ends + c, per, stride=band * ends), :] = total_ref[c, b]
    basis_ref[...] = turned_ref[...]


def fits(narrow, wide, shape, rank, width):
    order, rows_two, rows_three, cells = shape
    return (
        rank == narrow * SUBLANES
        and width % wide == 0
        and wide % 2 == 0
        and order % (narrow * wide * SUBLANES) == 0
        and rows_two * rows_three % 32 == 0
        and rows_two * rows_three >= 32 * DEPTH
        and rows_two % SUBLANES == 0
        and order * rows_two * rows_three * cells * 4 >= 64 << 20
    )


def fused(narrow, wide, table, prior, two, three):
    order, rows_two, depth, cells = table.shape
    rank, width, ends = prior.shape[1], two.shape[1], three.shape[1]
    rows = rows_two * depth
    tall = order // SUBLANES
    block = 32
    padded = block + SUBLANES
    groups = narrow // 2 * wide
    eight = order // (2 * groups)
    per, band, chips = rank // narrow, width // wide, narrow // 2
    lines_z = depth * width * (order + 1)
    slots = max(-(-lines_z // (tall * padded)), DEPTH * SUBLANES)
    share, half = order // PARTS, width // 2
    dma = pltpu.SemaphoreType.DMA
    anywhere = pl.BlockSpec(memory_space=pl.ANY)
    local = pl.BlockSpec(memory_space=pltpu.VMEM)
    turned, total = pl.pallas_call(
        functools.partial(fused_kernel, narrow, wide, 1.0 / float(I2 * I3 * M)),
        in_specs=[anywhere] * 5,
        out_specs=[local, local],
        out_shape=[
            jax.ShapeDtypeStruct((rank, order), F32),
            jax.ShapeDtypeStruct((ends, band, per, cells), F32),
        ],
        scratch_shapes=[
            pltpu.VMEM((rank, order), F32),
            pltpu.VMEM((width, two.shape[0]), F32),
            pltpu.SMEM((ends, three.shape[0]), F32),
            pltpu.VMEM((slots, tall, padded, cells), F32),
            pltpu.VMEM((RING, share, rows_two, cells), F32),
            pltpu.VMEM((order, order), F32),
            pltpu.VMEM((order, order), F32),
            pltpu.VMEM((2, groups, eight, order), F32),
            pltpu.VMEM((groups, eight, order), F32),
            pltpu.VMEM((2, groups, eight, order), F32),
            pltpu.VMEM((depth, 2, 2, chips, half, per, cells), F32),
            pltpu.VMEM((depth, 2, chips, half, per, cells), F32),
            pltpu.VMEM((depth, 2, chips, half, per, cells), F32),
            pltpu.VMEM((depth, wide, band, per, cells), F32),
            dma((3,)), dma((DEPTH, SUBLANES)), dma((RING,)),
            *[dma((1,))] * 8,
            dma((depth, 2)), dma((depth, 2)),
            dma((depth, 2, chips)), dma((depth, 2, chips)),
            dma((depth,)), dma((depth,)),
        ],
        compiler_params=pltpu.CompilerParams(
            vmem_limit_bytes=60 << 20, collective_id=3, has_side_effects=True
        ),
    )(table.reshape(tall, SUBLANES, rows, cells), table, prior.T, two.T, three.T)
    core_out, turned = pl.pallas_call(
        finish_kernel,
        in_specs=[local, local],
        out_specs=[local, local],
        out_shape=[
            jax.ShapeDtypeStruct((per, band, ends, cells), F32),
            jax.ShapeDtypeStruct((rank, order), F32),
        ],
    )(total, turned)
    return core_out, turned.T


def per_device(narrow, wide, table, prior_one, factor_two, factor_three):
    order, rows_two, rows_three, cells = table.shape
    if fits(narrow, wide, table.shape, prior_one.shape[1], factor_two.shape[1]):
        return fused(narrow, wide, table, prior_one, factor_two, factor_three)
    flat = table.reshape(order, rows_two * rows_three, cells)
    turned = basis_of(narrow, wide, gram_of(flat), prior_one)
    at = lax.axis_index("narrow")
    two = lax.dynamic_slice_in_dim(factor_two, at * rows_two, rows_two, 0).T
    spread = project(narrow, wide, turned, two, flat, rows_three)
    three = factor_three.reshape(wide, rows_three, factor_three.shape[1])
    core_out = jnp.einsum("wrbjm,wjc->rbcm", spread, three, precision=HIGH)
    return core_out, turned.T


def solution(mesh):
    return jax.shard_map(
        functools.partial(per_device, mesh.shape["narrow"], mesh.shape["wide"]),
        mesh=mesh,
        in_specs=(P(None, "narrow", "wide", None), P(), P(), P()),
        out_specs=(P("narrow", "wide", None, None), P()),
        check_vma=False,
    )
```
